768 devices in a mesh: energy: 96 (over x, z, core), atom: 8 (over y).
Axes of the slice: x: 4, y: 8, z: 12, core: 2. Of those that a mesh axis runs over, the one named last changes fastest.
Arguments:
- green_blocks: bfloat16 [192, 16, 2, 256, 256], P('energy', 'atom'), may hold values from -6 to 6
- coupling: bfloat16 [16, 256, 256], P('atom'), may hold values from -0.375 to 0.375
- up_partner: int32 [192], P('energy'), may hold values from -1 to 191, as said below
- down_partner: int32 [192], P('energy'), may hold values from -1 to 189, as said below
- up_weight: float32 [192], P('energy'), may hold values from 0.3 to 1.2
- down_weight: float32 [192], P('energy'), may hold values from 0.3 to 1.2
- neighbours: int32 [16, 5], replicated, may hold values from -1 to 15, as said below
- strength: float32 [16, 5], replicated, may hold values from 0.3 to 1
Outputs:
- updated: bfloat16 [192, 16, 2, 256, 256], P('energy', 'atom')
The draws below stay inside these ranges and needn't reach their ends.
Inputs may be any that keep to these rules, and one draw needn't show every extreme that they name: up_partner[e] = e + k with 2 <= k <= 4, or -1 only where such an e + k would pass the last energy point; k = 4 for some e. down_partner[e] = e - k with 2 <= k <= 4, or -1 only where such an e - k would fall below 0; k = 4 for some e. neighbours[a, j] is a + j - 2 or -1; it is -1 where a + j - 2 lies outside the clusters, and for j = 1, 2, 3 it is -1 nowhere else.
All inputs are finite; a program needn't handle non-finite values.
Results may differ from the reference program's by a relative error of at most 0.023.
Values may be sent and summed in bfloat16 or wider, within the bound.
A program may use at most 32 MiB of HBM per device.

```python
import math
import jax
import jax.numpy as jnp
from jax import lax

ORB = 256
E_DEV = 2
NBR = 5
ENERGIES = 192
CLUSTERS = 16


def draw_up_partner(key, part):
    stride = jax.random.randint(jax.random.fold_in(key, 11), (ENERGIES,), E_DEV, 2 * E_DEV + 1)
    places = jnp.arange(ENERGIES, dtype=jnp.int32)
    stride = jnp.where(places == 0, 2 * E_DEV, stride)
    stride = jnp.where(places == ENERGIES - E_DEV - 1, E_DEV, stride)
    target = places + stride
    return jnp.where(target < ENERGIES, target, -1).astype(jnp.int32)


def draw_down_partner(key, part):
    stride = jax.random.randint(jax.random.fold_in(key, 23), (ENERGIES,), E_DEV, 2 * E_DEV + 1)
    places = jnp.arange(ENERGIES, dtype=jnp.int32)
    stride = jnp.where(places == 2 * E_DEV, 2 * E_DEV, stride)
    stride = jnp.where(places == ENERGIES - 1, E_DEV, stride)
    target = places - stride
    return jnp.where(target >= 0, target, -1).astype(jnp.int32)


def draw_neighbours(key, part):
    present = jax.random.randint(jax.random.fold_in(key, 37), (CLUSTERS, NBR), 0, 2)
    slots = jnp.arange(NBR, dtype=jnp.int32)
    always = (slots >= 1) & (slots <= 3)
    present = jnp.where(always[None, :], 1, present)
    target = jnp.arange(CLUSTERS, dtype=jnp.int32)[:, None] + slots[None, :] - 2
    inside = (target >= 0) & (target < CLUSTERS)
    return jnp.where(inside & (present == 1), target, -1).astype(jnp.int32)


def steps_of(key, extent, cuts, smallest, top_value):
    gain, own = 1.0, jax.random.fold_in(key, 6)
    for axis_at, blocks in cuts:
        steps = jnp.exp(jax.random.uniform(jax.random.fold_in(own, axis_at), (blocks,), jnp.float32, smallest / len(cuts), top_value / len(cuts)))
        gain = gain * jnp.repeat(steps, extent[axis_at] // blocks).reshape([-1 if axis == axis_at else 1 for axis in range(len(extent))])
    return gain


def bell_draw(key, extent, width, reach, cuts=(), held_as=jnp.bfloat16):
    level = steps_of(key, extent, cuts, -0.22, 0.18) if cuts else 1.0
    entries = jax.random.normal(key, extent, jnp.float32) * width * level
    return jnp.minimum(jnp.maximum(entries, -reach), reach).astype(held_as)


def setup_inputs(seed: int = 0) -> dict:
    key_of = jax.random.split(jax.random.key(seed), 9)
    green_blocks = bell_draw(key_of[0], (ENERGIES, CLUSTERS, 2, ORB, ORB), 1.0, 6.0, ((0, 96), (1, 8)))
    coupling = bell_draw(key_of[1], (CLUSTERS, ORB, ORB), ORB ** -0.5, 0.375, ((0, 8),))
    up_partner = draw_up_partner(jax.random.fold_in(key_of[8], 71), 0)
    down_partner = draw_down_partner(jax.random.fold_in(key_of[8], 71), 0)
    up_weight = jnp.clip(jnp.exp(math.log(1.2) - 1.3862944 * jax.random.uniform(key_of[4], (ENERGIES,), jnp.float32) ** steps_of(key_of[4], (ENERGIES,), ((0, 96),), -0.2, 0.2)), 0.3, 1.2)
    down_weight = jnp.clip(jnp.exp(math.log(1.2) - 1.3862944 * jax.random.uniform(key_of[5], (ENERGIES,), jnp.float32) ** steps_of(key_of[5], (ENERGIES,), ((0, 96),), -0.2, 0.2)), 0.3, 1.2)
    neighbours = draw_neighbours(jax.random.fold_in(key_of[8], 71), 0)
    strength = jnp.clip(jnp.exp(jax.random.uniform(key_of[7], (CLUSTERS, NBR), jnp.float32, math.log(0.3), math.log(1.0))), 0.3, 1.0)
    return {"green_blocks": green_blocks, "coupling": coupling, "up_partner": up_partner, "down_partner": down_partner, "up_weight": up_weight, "down_weight": down_weight, "neighbours": neighbours, "strength": strength}


def complex_product(left, right):
    left_f = left.astype(jnp.float32)
    right_f = right.astype(jnp.float32)
    real_part = jnp.einsum('cij,cjk->cik', left_f[:, 0], right_f[:, 0]) - jnp.einsum('cij,cjk->cik', left_f[:, 1], right_f[:, 1])
    imag_part = jnp.einsum('cij,cjk->cik', left_f[:, 0], right_f[:, 1]) + jnp.einsum('cij,cjk->cik', left_f[:, 1], right_f[:, 0])
    return jnp.stack([real_part, imag_part], axis=1)


def reference(green_blocks, coupling, up_partner, down_partner, up_weight, down_weight, neighbours, strength):
    columns = jnp.arange(CLUSTERS, dtype=jnp.int32)
    coupling_table = jnp.sum(strength[:, :, None] * (neighbours[:, :, None] == columns[None, None, :]).astype(jnp.float32), axis=1)
    coupling_f = coupling.astype(jnp.float32)
    prefactor = 1.0 / (2.0 * ORB)

    def one_energy(energy_at):
        upper = up_partner[energy_at]
        lower = down_partner[energy_at]
        upper_factor = jnp.where(upper >= 0, up_weight[energy_at], jnp.float32(0.0))
        lower_factor = jnp.where(lower >= 0, down_weight[energy_at], jnp.float32(0.0))
        upper_block = green_blocks[jnp.maximum(upper, 0).astype(jnp.int32)].astype(jnp.float32)
        lower_block = green_blocks[jnp.maximum(lower, 0).astype(jnp.int32)].astype(jnp.float32)
        hidden = (upper_factor * upper_block + lower_factor * lower_block).astype(jnp.bfloat16)
        reader_sum = jnp.einsum('ab,bcij->acij', coupling_table, hidden.astype(jnp.float32)).astype(jnp.bfloat16)
        half_product = jnp.einsum('aij,acjk->acik', coupling_f, reader_sum.astype(jnp.float32)).astype(jnp.bfloat16)
        self_energy = (jnp.einsum('acij,akj->acik', half_product.astype(jnp.float32), coupling_f) * prefactor).astype(jnp.bfloat16)
        own_block = green_blocks[energy_at]
        first_term = complex_product(self_energy, own_block).astype(jnp.bfloat16)
        second_term = complex_product(own_block, first_term)
        second_rounded = second_term.astype(jnp.bfloat16)
        third_term = complex_product(second_rounded, first_term)
        return (own_block.astype(jnp.float32) + second_term + third_term).astype(jnp.bfloat16)

    return lax.map(one_energy, jnp.arange(ENERGIES, dtype=jnp.int32))
```

```python
import functools

import jax
import jax.numpy as jnp
from jax import lax
from jax.experimental import pallas as pl
from jax.experimental.pallas import tpu as pltpu
from jax.sharding import PartitionSpec as P

MESH = pl.DeviceIdType.MESH
CHUNKS = 4
F32 = jnp.float32
BF16 = jnp.bfloat16

TO_LOW, TO_HIGH, OWN, PASSED, TO_UNDER, TO_OVER = range(6)


def kernel(
    energy_devices,
    atom_devices,
    green_hbm,
    coupling_hbm,
    up_hbm,
    down_hbm,
    up_weight_hbm,
    down_weight_hbm,
    neighbours_hbm,
    strength_hbm,
    out_hbm,
    *scratch,
):
    chunks = CHUNKS
    orbitals = green_hbm.shape[-1]
    rows = orbitals // chunks
    names = iter(scratch)

    def take(count):
        return [next(names) for _ in range(count)]

    raw_z = take(chunks)
    raw_y = take(chunks)
    summed_z = [take(chunks) for _ in range(2)]
    summed_y = [take(chunks) for _ in range(2)]
    own_sum = [take(chunks) for _ in range(2)]
    hidden = take(chunks)
    sent_y = [take(chunks) for _ in range(2)]
    (
        green,
        coupling,
        up,
        down,
        up_weight,
        down_weight,
        neighbours,
        strength,
        reader,
        x_big,
        gc,
        y_big,
        f_big,
        second_cat,
        result,
        raw_send,
        raw_recv,
        sum_send,
        sum_recv,
        local_sem,
        out_sem,
    ) = names

    d = lax.axis_index("energy")
    y = lax.axis_index("atom")
    core = lax.rem(d, 2)
    low = lax.rem(d + energy_devices - 2, energy_devices)
    high = lax.rem(d + 2, energy_devices)
    partner = d + 1 - 2 * core
    under = lax.rem(y + atom_devices - 1, atom_devices)
    over = lax.rem(y + 1, atom_devices)
    targets = {
        TO_LOW: (low, y),
        TO_HIGH: (high, y),
        OWN: (partner, y),
        PASSED: (partner, y),
        TO_UNDER: (d, under),
        TO_OVER: (d, over),
    }
    slot_of = {TO_LOW: 6, TO_HIGH: 0, OWN: 2 + 2 * core, PASSED: 4 - 2 * core}
    passed_from = 6 - 6 * core

    def remote(source, target, send, recv, kind):
        return pltpu.make_async_remote_copy(
            src_ref=source,
            dst_ref=target,
            send_sem=send,
            recv_sem=recv,
            device_id=targets[kind],
            device_id_type=MESH,
        )

    def raw_copy(kind, r):
        send, recv = raw_send.at[kind, r], raw_recv.at[kind, r]
        if kind in (TO_UNDER, TO_OVER):
            source = green_hbm.at[:, :, 1, pl.ds(r * rows, rows), :]
            side = 1 if kind == TO_UNDER else 0
            return remote(source, raw_y[r].at[side], send, recv, kind)
        target = raw_z[r].at[pl.ds(slot_of[kind], 2)]
        if kind == PASSED:
            source = raw_z[r].at[pl.ds(passed_from, 2)]
        else:
            source = green_hbm.at[:, :, 0, pl.ds(r * rows, rows), :]
        return remote(source, target, send, recv, kind)

    def sum_copy(kind, a, r):
        index = a * chunks + r
        send, recv = sum_send.at[kind, index], sum_recv.at[kind, index]
        if kind in (TO_UNDER, TO_OVER):
            side = 1 if kind == TO_UNDER else 0
            return remote(
                sent_y[a][r].at[1 - side], summed_y[a][r].at[side], send, recv, kind
            )
        target = summed_z[a][r].at[pl.ds(slot_of[kind], 2)]
        if kind == PASSED:
            source = summed_z[a][r].at[pl.ds(passed_from, 2)]
        else:
            source = own_sum[a][r]
        return remote(source, target, send, recv, kind)

    locals_ = [
        pltpu.make_async_copy(source, target, local_sem.at[i])
        for i, (source, target) in enumerate(
            (
                (coupling_hbm, coupling),
                (green_hbm, green),
                (up_hbm, up),
                (down_hbm, down),
                (up_weight_hbm, up_weight),
                (down_weight_hbm, down_weight),
                (neighbours_hbm, neighbours),
                (strength_hbm, strength),
            )
        )
    ]
    for copy in locals_:
        copy.start()

    barrier = pltpu.get_barrier_semaphore()
    for kind in (TO_LOW, TO_HIGH, OWN, TO_UNDER, TO_OVER):
        pl.semaphore_signal(barrier, inc=1, device_id=targets[kind], device_id_type=MESH)
    pl.semaphore_wait(barrier, 5)

    for r in range(chunks):
        for kind in (TO_LOW, TO_HIGH, TO_UNDER, TO_OVER, OWN):
            raw_copy(kind, r).start()

    for copy in locals_:
        copy.wait()

    clusters = 2 * atom_devices
    first_energy = 2 * d
    first_cluster = 2 * y

    def table(a, b):
        row = lax.rem(a + clusters, clusters)
        inside = (a >= 0) & (a < clusters) & (b >= 0) & (b < clusters)
        total = jnp.float32(0.0)
        for j in range(neighbours.shape[0]):
            total = total + jnp.where(neighbours[j, row] == b, strength[j, row], jnp.float32(0.0))
        return jnp.where(inside, total, jnp.float32(0.0))

    def entry(a, b):
        return table(first_cluster + a, first_cluster + b)

    reach = {
        (a, b): entry(a, b) for a in range(-2, 4) for b in range(-2, 4)
        if abs(a - b) <= 2 and (0 <= a < 2 or 0 <= b < 2)
    }

    up_slot, down_slot, up_factor, down_factor = [], [], [], []
    for e in range(2):
        u, l = up[e], down[e]
        up_slot.append(jnp.minimum(jnp.maximum(u - first_energy + 2, 4), 7))
        down_slot.append(jnp.minimum(jnp.maximum(l - first_energy + 4, 0), 3))
        up_factor.append(jnp.where(u >= 0, up_weight[e], jnp.float32(0.0)))
        down_factor.append(jnp.where(l >= 0, down_weight[e], jnp.float32(0.0)))

    def dot(left, right):
        return jnp.dot(left, right, preferred_element_type=F32)

    scale = 1.0 / (2.0 * orbitals)
    for a in range(2):
        turned = coupling[a].T
        for e in range(2):
            for part in range(2):
                x = dot(turned, green[e, a, part]) * scale
                x_big[a, e, 0:orbitals, part * orbitals : (part + 1) * orbitals] = x.astype(BF16)
                other = -x if part == 1 else x
                x_big[a, e, orbitals:, (1 - part) * orbitals : (2 - part) * orbitals] = other.astype(BF16)
                gc[a, e, :, part * orbitals : (part + 1) * orbitals] = dot(
                    green[e, a, part], coupling[a]
                ).astype(BF16)

    def wide(value):
        return value.astype(F32)

    def cluster_sums(r):
        span = pl.ds(r * rows, rows)
        for e in range(2):
            terms = {
                -2: wide(raw_y[r][0, e, 0]),
                -1: wide(raw_y[r][0, e, 1]),
                0: wide(green[e, 0, 1, span, :]),
                1: wide(green[e, 1, 1, span, :]),
                2: wide(raw_y[r][1, e, 0]),
                3: wide(raw_y[r][1, e, 1]),
            }
            for a in range(2):
                total = None
                for b in range(a - 2, a + 3):
                    piece = reach[a, b] * terms[b]
                    total = piece if total is None else total + piece
                own_sum[a][r][e] = total.astype(BF16)

    def energy_sums(r):
        for e in range(2):
            values = []
            for c in range(2):
                value = (
                    up_factor[e] * wide(raw_z[r][up_slot[e], c])
                    + down_factor[e] * wide(raw_z[r][down_slot[e], c])
                ).astype(BF16)
                hidden[r][e, c] = value
                values.append(wide(value))
            sent_y[0][r][0, e] = (reach[-2, 0] * values[0]).astype(BF16)
            sent_y[1][r][0, e] = (reach[-1, 0] * values[0] + reach[-1, 1] * values[1]).astype(BF16)
            sent_y[0][r][1, e] = (reach[2, 0] * values[0] + reach[2, 1] * values[1]).astype(BF16)
            sent_y[1][r][1, e] = (reach[3, 1] * values[1]).astype(BF16)

    def energy_sum_send(a, r):
        for kind in (TO_UNDER, TO_OVER):
            sum_copy(kind, a, r).start()

    def cluster_sum_send(a, r):
        for kind in (TO_LOW, TO_HIGH, OWN):
            sum_copy(kind, a, r).start()

    def raw_second(r):
        raw_copy(OWN, r).wait_recv()
        raw_copy(PASSED, r).wait_recv()
        energy_sums(r)
        energy_sum_send(0, r)

    for r in range(chunks):
        raw_copy(TO_LOW, r).wait_recv()
        raw_copy(TO_HIGH, r).wait_recv()
        raw_copy(PASSED, r).start()
        if r:
            raw_second(r - 1)
        raw_copy(TO_UNDER, r).wait_recv()
        raw_copy(TO_OVER, r).wait_recv()
        cluster_sums(r)
        cluster_sum_send(0, r)
    for r in range(chunks):
        cluster_sum_send(1, r)
    raw_second(chunks - 1)
    for r in range(chunks):
        energy_sum_send(1, r)

    def read(a, r):
        span = pl.ds(r * rows, rows)
        for kind in (TO_UNDER, TO_OVER):
            sum_copy(kind, a, r).wait_recv()
        for e in range(2):
            total = wide(summed_y[a][r][0, e]) + wide(summed_y[a][r][1, e])
            for c in range(2):
                total = total + reach[a, c] * wide(hidden[r][e, c])
            reader[a, e, :, 0:orbitals] = total.astype(BF16)
        for kind in (OWN, PASSED):
            sum_copy(kind, a, r).wait_recv()
        for e in range(2):
            total = up_factor[e] * wide(summed_z[a][r][up_slot[e]]) + down_factor[e] * wide(
                summed_z[a][r][down_slot[e]]
            )
            reader[a, e, :, orbitals:] = total.astype(BF16)
        for e in range(2):
            value = dot(reader[a, e], x_big[a, e])
            real, imag = value[:, :orbitals].astype(BF16), value[:, orbitals:].astype(BF16)
            after = pl.ds(orbitals + r * rows, rows)
            y_big[a, e, span, 0:orbitals] = real
            y_big[a, e, span, orbitals:] = imag
            y_big[a, e, after, 0:orbitals] = -imag
            y_big[a, e, after, orbitals:] = real

    def finish(a):
        for e in range(2):
            first = dot(coupling[a], y_big[a, e, 0:orbitals])
            real, imag = first[:, :orbitals].astype(BF16), first[:, orbitals:].astype(BF16)
            f_big[e, 0:orbitals, 0:orbitals] = real
            f_big[e, 0:orbitals, orbitals:] = imag
            f_big[e, orbitals:, 0:orbitals] = -imag
            f_big[e, orbitals:, orbitals:] = real
        for e in range(2):
            second_cat[e] = dot(gc[a, e], y_big[a, e])
        for e in range(2):
            third = dot(second_cat[e].astype(BF16), f_big[e])
            for part in range(2):
                side = slice(part * orbitals, (part + 1) * orbitals)
                result[a, e, part] = (
                    wide(green[e, a, part]) + second_cat[e, :, side] + third[:, side]
                ).astype(BF16)
        for e in range(2):
            out_copy(a, e).start()

    def out_copy(a, e):
        return pltpu.make_async_copy(result.at[a, e], out_hbm.at[e, a], out_sem.at[a, e])

    steps = [(a, r) for a in range(2) for r in range(chunks)]
    for at, (a, r) in enumerate(steps):
        sum_copy(TO_LOW, a, r).wait_recv()
        sum_copy(TO_HIGH, a, r).wait_recv()
        sum_copy(PASSED, a, r).start()
        if at:
            read(*steps[at - 1])
            if steps[at - 1][1] == chunks - 1:
                finish(steps[at - 1][0])
    read(*steps[-1])
    finish(1)

    for r in range(chunks):
        for kind in range(6):
            raw_copy(kind, r).wait_send()
            for a in range(2):
                sum_copy(kind, a, r).wait_send()
    for a in range(2):
        for e in range(2):
            out_copy(a, e).wait()


def solution(mesh):
    energy_devices, atom_devices = mesh.shape["energy"], mesh.shape["atom"]

    def on_device(
        green_blocks, coupling, up_partner, down_partner, up_weight, down_weight, neighbours, strength
    ):
        orbitals = green_blocks.shape[-1]
        rows = orbitals // CHUNKS
        slots = neighbours.shape[1]
        clusters = neighbours.shape[0]

        def vmem(*shape, dtype=BF16):
            return pltpu.VMEM(shape, dtype)

        many = range(CHUNKS)
        scratch = (
            [vmem(8, 2, rows, orbitals) for _ in many]
            + [vmem(2, 2, 2, rows, orbitals) for _ in many]
            + [vmem(8, rows, orbitals) for _ in range(2 * CHUNKS)]
            + [vmem(2, 2, rows, orbitals) for _ in range(2 * CHUNKS)]
            + [vmem(2, rows, orbitals) for _ in range(2 * CHUNKS)]
            + [vmem(2, 2, rows, orbitals) for _ in many]
            + [vmem(2, 2, rows, orbitals) for _ in range(2 * CHUNKS)]
            + [
                vmem(2, 2, 2, orbitals, orbitals),
                vmem(2, orbitals, orbitals),
                pltpu.SMEM((2,), jnp.int32),
                pltpu.SMEM((2,), jnp.int32),
                pltpu.SMEM((2,), F32),
                pltpu.SMEM((2,), F32),
                pltpu.SMEM((slots, clusters), jnp.int32),
                pltpu.SMEM((slots, clusters), F32),
                vmem(2, 2, rows, 2 * orbitals),
                vmem(2, 2, 2 * orbitals, 2 * orbitals),
                vmem(2, 2, orbitals, 2 * orbitals),
                vmem(2, 2, 2 * orbitals, 2 * orbitals),
                vmem(2, 2 * orbitals, 2 * orbitals),
                vmem(2, orbitals, 2 * orbitals, dtype=F32),
                vmem(2, 2, 2, orbitals, orbitals),
                pltpu.SemaphoreType.DMA((6, CHUNKS)),
                pltpu.SemaphoreType.DMA((6, CHUNKS)),
                pltpu.SemaphoreType.DMA((6, 2 * CHUNKS)),
                pltpu.SemaphoreType.DMA((6, 2 * CHUNKS)),
                pltpu.SemaphoreType.DMA((8,)),
                pltpu.SemaphoreType.DMA((2, 2)),
            ]
        )
        return pl.pallas_call(
            functools.partial(kernel, energy_devices, atom_devices),
            out_shape=jax.ShapeDtypeStruct(green_blocks.shape, green_blocks.dtype),
            in_specs=[pl.BlockSpec(memory_space=pl.ANY)] * 8,
            out_specs=pl.BlockSpec(memory_space=pl.ANY),
            scratch_shapes=scratch,
            compiler_params=pltpu.CompilerParams(
                collective_id=0, has_side_effects=True, vmem_limit_bytes=60 * 1024 * 1024
            ),
            name="update",
        )(
            green_blocks,
            coupling,
            up_partner,
            down_partner,
            up_weight,
            down_weight,
            neighbours.T,
            strength.T,
        )

    in_specs = (
        P("energy", "atom", None, None, None),
        P("atom", None, None),
        P("energy"),
        P("energy"),
        P("energy"),
        P("energy"),
        P(),
        P(),
    )
    out_specs = P("energy", "atom", None, None, None)
    return jax.shard_map(
        on_device, mesh=mesh, in_specs=in_specs, out_specs=out_specs, check_vma=False
    )
```

```python
import functools

import jax
import jax.numpy as jnp
from jax import lax
from jax.experimental import pallas as pl
from jax.experimental.pallas import tpu as pltpu
from jax.sharding import PartitionSpec as P

MESH = pl.DeviceIdType.MESH
CHUNKS = 4
ROW = 24
F32 = jnp.float32
BF16 = jnp.bfloat16

TO_LOW, TO_HIGH, OWN, PASSED, TO_UNDER, TO_OVER = range(6)
OVER_Z = (TO_LOW, TO_HIGH, OWN)
OVER_Y = (TO_UNDER, TO_OVER)
scope = jax.named_scope


def kernel(
    energy_devices,
    atom_devices,
    green_hbm,
    coupling_hbm,
    up_hbm,
    down_hbm,
    up_weight_hbm,
    down_weight_hbm,
    neighbours_hbm,
    strength_hbm,
    out_ref,
    *scratch,
):
    chunks = CHUNKS
    orbitals = green_hbm.shape[-1]
    rows = orbitals // chunks
    names = iter(scratch)

    def take(count):
        return [next(names) for _ in range(count)]

    raw_z = take(chunks)
    raw_y = take(chunks)
    summed_z = [take(chunks) for _ in range(2)]
    summed_y = [take(chunks) for _ in range(2)]
    own_sum = [take(chunks) for _ in range(2)]
    hidden = take(chunks)
    sent_y = [take(chunks) for _ in range(2)]
    (
        green,
        coupling,
        up,
        down,
        up_weight,
        down_weight,
        neighbours,
        strength,
        reader,
        x_big,
        gc,
        y_big,
        f_big,
        second_cat,
        raw_send,
        raw_recv,
        sum_send,
        sum_recv,
        local_sem,
        ready,
    ) = names

    d = lax.axis_index("energy")
    y = lax.axis_index("atom")
    core = lax.rem(d, 2)
    has_low, has_high = d >= 2, d < energy_devices - 2
    has_under, has_over = y >= 1, y < atom_devices - 1
    exists = {
        TO_LOW: has_low,
        TO_HIGH: has_high,
        OWN: d >= 0,
        TO_UNDER: has_under,
        TO_OVER: has_over,
    }
    partner = d + 1 - 2 * core
    targets = {
        TO_LOW: (d - 2, y),
        TO_HIGH: (d + 2, y),
        OWN: (partner, y),
        PASSED: (partner, y),
        TO_UNDER: (d, y - 1),
        TO_OVER: (d, y + 1),
    }
    place = lax.rem(d, ROW)
    never = d < 0
    first = (d == 0) & (y == 0)
    leads = {
        TO_LOW: never,
        TO_HIGH: first | (place >= ROW - 2),
        OWN: first,
        TO_UNDER: never,
        TO_OVER: first,
    }
    late = {
        TO_LOW: ((d == 2) & (y == 0)) | ((place < 2) & (d >= ROW)),
        TO_HIGH: never,
        OWN: (d == 1) & (y == 0),
        TO_UNDER: (d == 0) & (y == 1),
        TO_OVER: never,
    }
    meets_z = late[TO_LOW] | late[OWN]
    slow_high = (place >= ROW - 2) & has_high
    late_z = meets_z | slow_high
    early_core = jnp.where(slow_high, 1, 0)
    late_y = late[TO_UNDER]
    pass_out = jnp.where(core == 0, d < energy_devices - 2, d >= 2)
    pass_in = jnp.where(core == 0, d >= 2, d < energy_devices - 2)
    slot_of = {TO_LOW: 6, TO_HIGH: 0, OWN: 2 + 2 * core, PASSED: 4 - 2 * core}
    passed_from = 6 - 6 * core
    kept_from = 6 * core

    barrier = pltpu.get_barrier_semaphore()
    count = jnp.int32(0)
    for kind in (TO_LOW, TO_HIGH, OWN, TO_UNDER, TO_OVER):
        count = count + jnp.where(exists[kind], 1, 0) - jnp.where(late[kind], 1, 0)

        @pl.when(exists[kind] & jnp.logical_not(leads[kind]))
        def _(kind=kind):
            pl.semaphore_signal(barrier, inc=1, device_id=targets[kind], device_id_type=MESH)

    def remote(source, target, send, recv, kind):
        return pltpu.make_async_remote_copy(
            src_ref=source,
            dst_ref=target,
            send_sem=send,
            recv_sem=recv,
            device_id=targets[kind],
            device_id_type=MESH,
        )

    def raw_copy(kind, r):
        send, recv = raw_send.at[kind, r], raw_recv.at[kind, r]
        if kind in (TO_UNDER, TO_OVER):
            source = green.at[:, :, 1, pl.ds(r * rows, rows), :]
            side = 1 if kind == TO_UNDER else 0
            return remote(source, raw_y[r].at[side], send, recv, kind)
        target = raw_z[r].at[pl.ds(slot_of[kind], 2)]
        if kind == PASSED:
            source = raw_z[r].at[pl.ds(passed_from, 2)]
        else:
            source = green.at[:, :, 0, pl.ds(r * rows, rows), :]
        return remote(source, target, send, recv, kind)

    def sum_copy(kind, a, r):
        index = a * chunks + r
        send, recv = sum_send.at[kind, index], sum_recv.at[kind, index]
        if kind in (TO_UNDER, TO_OVER):
            side = 1 if kind == TO_UNDER else 0
            return remote(
                sent_y[a][r].at[1 - side], summed_y[a][r].at[side], send, recv, kind
            )
        target = summed_z[a][r].at[pl.ds(slot_of[kind], 2)]
        if kind == PASSED:
            source = summed_z[a][r].at[pl.ds(passed_from, 2)]
        else:
            source = own_sum[a][r]
        return remote(source, target, send, recv, kind)

    def raw_arrival(r, start, which):
        place = raw_z[r].at[pl.ds(start, 2)]
        return remote(place, place, raw_send.at[which, r], raw_recv.at[which, r], OWN)

    def sum_arrival(a, r, start, which):
        place, index = summed_z[a][r].at[pl.ds(start, 2)], a * chunks + r
        return remote(place, place, sum_send.at[which, index], sum_recv.at[which, index], OWN)

    locals_ = [
        pltpu.make_async_copy(source, target, local_sem.at[i])
        for i, (source, target) in enumerate(
            (
                (green_hbm, green),
                (coupling_hbm, coupling),
                (up_hbm, up),
                (down_hbm, down),
                (up_weight_hbm, up_weight),
                (down_weight_hbm, down_weight),
                (neighbours_hbm, neighbours),
                (strength_hbm, strength),
            )
        )
    ]
    for copy in locals_:
        copy.start()

    with scope("S_barrier"):
        pl.semaphore_wait(barrier, count)

    for kind in (TO_HIGH, OWN, TO_OVER):

        @pl.when(exists[kind] & leads[kind])
        def _(kind=kind):
            pl.semaphore_signal(ready, inc=1, device_id=targets[kind], device_id_type=MESH)

    locals_[0].wait()
    for kind in (TO_LOW, TO_HIGH, TO_UNDER, TO_OVER, OWN):

        @pl.when(exists[kind] & jnp.logical_not(late[kind]))
        def _(kind=kind):
            for r in range(chunks):
                raw_copy(kind, r).start()

    def clear(condition, refs):
        @pl.when(jnp.logical_not(condition))
        def _():
            for ref in refs:
                ref[...] = jnp.zeros(ref.shape, ref.dtype)

    flat_z = [ref for a in range(2) for ref in summed_z[a]]
    flat_y = [ref for a in range(2) for ref in summed_y[a]]
    clear(has_low, [ref.at[0:2] for ref in raw_z + flat_z])
    clear(has_high, [ref.at[6:8] for ref in raw_z + flat_z])
    clear(has_under, [ref.at[0] for ref in raw_y + flat_y])
    clear(has_over, [ref.at[1] for ref in raw_y + flat_y])

    with scope("S_localwait"):
        for copy in locals_[1:]:
            copy.wait()

    clusters = 2 * atom_devices
    first_energy = 2 * d
    first_cluster = 2 * y

    def table(a, b):
        row = lax.rem(a + clusters, clusters)
        inside = (a >= 0) & (a < clusters) & (b >= 0) & (b < clusters)
        total = jnp.float32(0.0)
        for j in range(neighbours.shape[0]):
            total = total + jnp.where(neighbours[j, row] == b, strength[j, row], jnp.float32(0.0))
        return jnp.where(inside, total, jnp.float32(0.0))

    def entry(a, b):
        return table(first_cluster + a, first_cluster + b)

    reach = {
        (a, b): entry(a, b) for a in range(-2, 4) for b in range(-2, 4)
        if abs(a - b) <= 2 and (0 <= a < 2 or 0 <= b < 2)
    }

    up_slot, down_slot, up_factor, down_factor = [], [], [], []
    for e in range(2):
        u, l = up[e], down[e]
        up_slot.append(jnp.where(u >= 0, jnp.minimum(jnp.maximum(u - first_energy + 2, 4), 7), 7))
        down_slot.append(jnp.where(l >= 0, jnp.minimum(jnp.maximum(l - first_energy + 4, 0), 3), 0))
        up_factor.append(jnp.where(u >= 0, up_weight[e], jnp.float32(0.0)))
        down_factor.append(jnp.where(l >= 0, down_weight[e], jnp.float32(0.0)))

    def dot(left, right):
        return jnp.dot(left, right, preferred_element_type=F32)

    scale = 1.0 / (2.0 * orbitals)
    for a in range(2):
        turned = coupling[a].T
        for e in range(2):
            for part in range(2):
                x = dot(turned, green[e, a, part]) * scale
                x_big[a, e, 0:orbitals, part * orbitals : (part + 1) * orbitals] = x.astype(BF16)
                other = -x if part == 1 else x
                x_big[a, e, orbitals:, (1 - part) * orbitals : (2 - part) * orbitals] = other.astype(BF16)
                gc[a, e, :, part * orbitals : (part + 1) * orbitals] = dot(
                    green[e, a, part], coupling[a]
                ).astype(BF16)

    def wide(value):
        return value.astype(F32)

    def cluster_sums(r):
        span = pl.ds(r * rows, rows)
        for e in range(2):
            terms = {
                -2: wide(raw_y[r][0, e, 0]),
                -1: wide(raw_y[r][0, e, 1]),
                0: wide(green[e, 0, 1, span, :]),
                1: wide(green[e, 1, 1, span, :]),
                2: wide(raw_y[r][1, e, 0]),
                3: wide(raw_y[r][1, e, 1]),
            }
            for a in range(2):
                total = None
                for b in range(a - 2, a + 3):
                    piece = reach[a, b] * terms[b]
                    total = piece if total is None else total + piece
                own_sum[a][r][e] = total.astype(BF16)

    def energy_sums(r):
        for e in range(2):
            values = []
            for c in range(2):
                value = (
                    up_factor[e] * wide(raw_z[r][up_slot[e], c])
                    + down_factor[e] * wide(raw_z[r][down_slot[e], c])
                ).astype(BF16)
                hidden[r][e, c] = value
                values.append(wide(value))
            sent_y[0][r][0, e] = (reach[-2, 0] * values[0]).astype(BF16)
            sent_y[1][r][0, e] = (reach[-1, 0] * values[0] + reach[-1, 1] * values[1]).astype(BF16)
            sent_y[0][r][1, e] = (reach[2, 0] * values[0] + reach[2, 1] * values[1]).astype(BF16)
            sent_y[1][r][1, e] = (reach[3, 1] * values[1]).astype(BF16)

    def start_sums(kinds, a, r, only=None):
        for kind in kinds:
            condition = exists[kind]
            if only is not None:
                condition = late[kind] if only else condition & jnp.logical_not(late[kind])

            @pl.when(condition)
            def _(kind=kind):
                sum_copy(kind, a, r).start()

    def pass_raw(r, whose=None):
        @pl.when(pass_out if whose is None else pass_out & (core == whose))
        def _():
            with scope(f"W_zraw{r}"):
                raw_arrival(r, passed_from, core).wait_recv()
            raw_copy(PASSED, r).start()

    def over_energies(r, only=None):
        with scope(f"W_own{r}"):
            raw_copy(OWN, r).wait_recv()

        @pl.when(pass_in)
        def _():
            with scope(f"W_pass{r}"):
                raw_arrival(r, kept_from, 1 - core).wait_recv()
                raw_copy(PASSED, r).wait_recv()

        energy_sums(r)
        start_sums(OVER_Y, 0, r, only)

    def over_clusters(r, only=None):
        with scope(f"W_yraw{r}"):

            @pl.when(has_over)
            def _():
                raw_copy(TO_UNDER, r).wait_recv()

            @pl.when(has_under)
            def _():
                raw_copy(TO_OVER, r).wait_recv()

        cluster_sums(r)
        start_sums(OVER_Z, 0, r, only)

    def meet(kinds):
        pl.semaphore_wait(ready, 1)
        for kind in kinds:

            @pl.when(late[kind])
            def _(kind=kind):
                for r in range(chunks):
                    raw_copy(kind, r).start()

    @pl.when(jnp.logical_not(late_y | late_z))
    def _():
        for r in range(chunks):
            pass_raw(r)
            if r:
                over_energies(r - 1)
            over_clusters(r)
        for r in range(chunks):
            start_sums(OVER_Z, 1, r)
        start_sums(OVER_Y, 1, 0)
        over_energies(chunks - 1)
        for r in range(1, chunks):
            start_sums(OVER_Y, 1, r)

    @pl.when(late_y)
    def _():
        for r in range(chunks):
            pass_raw(r)
            if r:
                over_energies(r - 1, False)
                if r == 1:
                    meet(OVER_Y)
                start_sums(OVER_Y, 0, r - 1, True)
        start_sums(OVER_Y, 1, 0)
        over_energies(chunks - 1)
        for r in range(1, chunks):
            start_sums(OVER_Y, 1, r)
        for r in range(chunks):
            over_clusters(r)
        for r in range(chunks):
            start_sums(OVER_Z, 1, r)

    @pl.when(late_z)
    def _():
        for r in range(chunks):
            pass_raw(r, early_core)
            over_clusters(r, False)
            if r == 0:

                @pl.when(meets_z)
                def _():
                    meet(OVER_Z)

            start_sums(OVER_Z, 0, r, True)
        for r in range(chunks):
            start_sums(OVER_Z, 1, r)
        for r in range(chunks):
            pass_raw(r, 1 - early_core)
            if r:
                over_energies(r - 1)
        start_sums(OVER_Y, 1, 0)
        over_energies(chunks - 1)
        for r in range(1, chunks):
            start_sums(OVER_Y, 1, r)

    def read(a, r):
        span = pl.ds(r * rows, rows)
        with scope(f"W_ysum{a}{r}"):

            @pl.when(has_over)
            def _():
                sum_copy(TO_UNDER, a, r).wait_recv()

            @pl.when(has_under)
            def _():
                sum_copy(TO_OVER, a, r).wait_recv()

        for e in range(2):
            total = wide(summed_y[a][r][0, e]) + wide(summed_y[a][r][1, e])
            for c in range(2):
                total = total + reach[a, c] * wide(hidden[r][e, c])
            reader[a, e, :, 0:orbitals] = total.astype(BF16)
        with scope(f"W_zpass{a}{r}"):
            sum_copy(OWN, a, r).wait_recv()

            @pl.when(pass_in)
            def _():
                sum_arrival(a, r, kept_from, 1 - core).wait_recv()
                sum_copy(PASSED, a, r).wait_recv()

        for e in range(2):
            total = up_factor[e] * wide(summed_z[a][r][up_slot[e]]) + down_factor[e] * wide(
                summed_z[a][r][down_slot[e]]
            )
            reader[a, e, :, orbitals:] = total.astype(BF16)
        for e in range(2):
            value = dot(reader[a, e], x_big[a, e])
            real, imag = value[:, :orbitals].astype(BF16), value[:, orbitals:].astype(BF16)
            after = pl.ds(orbitals + r * rows, rows)
            y_big[a, e, span, 0:orbitals] = real
            y_big[a, e, span, orbitals:] = imag
            y_big[a, e, after, 0:orbitals] = -imag
            y_big[a, e, after, orbitals:] = real

    def finish(a):
        for e in range(2):
            first = dot(coupling[a], y_big[a, e, 0:orbitals])
            real, imag = first[:, :orbitals].astype(BF16), first[:, orbitals:].astype(BF16)
            f_big[e, 0:orbitals, 0:orbitals] = real
            f_big[e, 0:orbitals, orbitals:] = imag
            f_big[e, orbitals:, 0:orbitals] = -imag
            f_big[e, orbitals:, orbitals:] = real
        for e in range(2):
            second_cat[e] = dot(gc[a, e], y_big[a, e])
        for e in range(2):
            third = dot(second_cat[e].astype(BF16), f_big[e])
            for part in range(2):
                side = slice(part * orbitals, (part + 1) * orbitals)
                out_ref[e, a, part] = (
                    wide(green[e, a, part]) + second_cat[e, :, side] + third[:, side]
                ).astype(BF16)

    steps = [(a, r) for a in range(2) for r in range(chunks)]
    for at, (a, r) in enumerate(steps):

        @pl.when(pass_out)
        def _(a=a, r=r):
            with scope(f"W_zsum{a}{r}"):
                sum_arrival(a, r, passed_from, core).wait_recv()
            sum_copy(PASSED, a, r).start()

        if at:
            read(*steps[at - 1])
            if steps[at - 1][1] == chunks - 1:
                finish(steps[at - 1][0])
    read(*steps[-1])
    with scope("S_finish1"):
        finish(1)

    with scope("S_sends"):
        for kind in range(6):

            @pl.when(pass_out if kind == PASSED else exists[kind])
            def _(kind=kind):
                for r in range(chunks):
                    raw_copy(kind, r).wait_send()
                    for a in range(2):
                        sum_copy(kind, a, r).wait_send()


def solution(mesh):
    energy_devices, atom_devices = mesh.shape["energy"], mesh.shape["atom"]

    def on_device(
        green_blocks, coupling, up_partner, down_partner, up_weight, down_weight, neighbours, strength
    ):
        orbitals = green_blocks.shape[-1]
        rows = orbitals // CHUNKS
        slots = neighbours.shape[1]
        clusters = neighbours.shape[0]

        def vmem(*shape, dtype=BF16):
            return pltpu.VMEM(shape, dtype)

        many = range(CHUNKS)
        scratch = (
            [vmem(8, 2, rows, orbitals) for _ in many]
            + [vmem(2, 2, 2, rows, orbitals) for _ in many]
            + [vmem(8, rows, orbitals) for _ in range(2 * CHUNKS)]
            + [vmem(2, 2, rows, orbitals) for _ in range(2 * CHUNKS)]
            + [vmem(2, rows, orbitals) for _ in range(2 * CHUNKS)]
            + [vmem(2, 2, rows, orbitals) for _ in many]
            + [vmem(2, 2, rows, orbitals) for _ in range(2 * CHUNKS)]
            + [
                vmem(2, 2, 2, orbitals, orbitals),
                vmem(2, orbitals, orbitals),
                pltpu.SMEM((2,), jnp.int32),
                pltpu.SMEM((2,), jnp.int32),
                pltpu.SMEM((2,), F32),
                pltpu.SMEM((2,), F32),
                pltpu.SMEM((slots, clusters), jnp.int32),
                pltpu.SMEM((slots, clusters), F32),
                vmem(2, 2, rows, 2 * orbitals),
                vmem(2, 2, 2 * orbitals, 2 * orbitals),
                vmem(2, 2, orbitals, 2 * orbitals),
                vmem(2, 2, 2 * orbitals, 2 * orbitals),
                vmem(2, 2 * orbitals, 2 * orbitals),
                vmem(2, orbitals, 2 * orbitals, dtype=F32),
                pltpu.SemaphoreType.DMA((6, CHUNKS)),
                pltpu.SemaphoreType.DMA((6, CHUNKS)),
                pltpu.SemaphoreType.DMA((6, 2 * CHUNKS)),
                pltpu.SemaphoreType.DMA((6, 2 * CHUNKS)),
                pltpu.SemaphoreType.DMA((8,)),
                pltpu.SemaphoreType.REGULAR,
            ]
        )
        return pl.pallas_call(
            functools.partial(kernel, energy_devices, atom_devices),
            out_shape=jax.ShapeDtypeStruct(green_blocks.shape, green_blocks.dtype),
            in_specs=[pl.BlockSpec(memory_space=pl.ANY)] * 8,
            out_specs=pl.BlockSpec(memory_space=pltpu.VMEM),
            scratch_shapes=scratch,
            compiler_params=pltpu.CompilerParams(
                collective_id=0, has_side_effects=True, vmem_limit_bytes=24 * 1024 * 1024
            ),
            name="update",
        )(
            *(
                pltpu.with_memory_space_constraint(array, pltpu.HBM)
                for array in (
                    green_blocks,
                    coupling,
                    up_partner,
                    down_partner,
                    up_weight,
                    down_weight,
                    neighbours.T,
                    strength.T,
                )
            )
        )

    in_specs = (
        P("energy", "atom", None, None, None),
        P("atom", None, None),
        P("energy"),
        P("energy"),
        P("energy"),
        P("energy"),
        P(),
        P(),
    )
    out_specs = P("energy", "atom", None, None, None)
    return jax.shard_map(
        on_device, mesh=mesh, in_specs=in_specs, out_specs=out_specs, check_vma=False
    )
```

```python
import functools

import jax
import jax.numpy as jnp
from jax import lax
from jax.experimental import pallas as pl
from jax.experimental.pallas import tpu as pltpu
from jax.sharding import PartitionSpec as P

MESH = pl.DeviceIdType.MESH
CHUNKS = 4
ROW = 24
F32 = jnp.float32
BF16 = jnp.bfloat16

TO_LOW, TO_HIGH, OWN, PASSED, TO_UNDER, TO_OVER = range(6)
OVER_Z = (TO_LOW, TO_HIGH, OWN)
OVER_Y = (TO_UNDER, TO_OVER)
scope = jax.named_scope


def kernel(
    energy_devices,
    atom_devices,
    green_hbm,
    coupling_hbm,
    up_hbm,
    down_hbm,
    up_weight_hbm,
    down_weight_hbm,
    neighbours_hbm,
    strength_hbm,
    out_ref,
    *scratch,
):
    chunks = CHUNKS
    orbitals = green_hbm.shape[-1]
    rows = orbitals // chunks
    names = iter(scratch)

    def take(count):
        return [next(names) for _ in range(count)]

    raw_z = take(chunks)
    raw_y = take(chunks)
    summed_z = [take(chunks) for _ in range(2)]
    summed_y = [take(chunks) for _ in range(2)]
    own_sum = [take(chunks) for _ in range(2)]
    hidden = take(chunks)
    relay_raw = dict(zip((chunks - 2, chunks - 1), take(2)))
    relay_sum = [take(2) for _ in range(2)]
    sent_y = [take(chunks) for _ in range(2)]
    (
        green,
        coupling,
        up,
        down,
        up_weight,
        down_weight,
        neighbours,
        strength,
        reader,
        x_big,
        gc,
        y_big,
        f_big,
        second_cat,
        sent,
        raw_recv,
        sum_recv,
        relay_send,
        relay_recv,
        local_sem,
        ready,
    ) = names

    d = lax.axis_index("energy")
    y = lax.axis_index("atom")
    core = lax.rem(d, 2)
    has_low, has_high = d >= 2, d < energy_devices - 2
    has_under, has_over = y >= 1, y < atom_devices - 1
    exists = {
        TO_LOW: has_low,
        TO_HIGH: has_high,
        OWN: d >= 0,
        TO_UNDER: has_under,
        TO_OVER: has_over,
    }
    partner = d + 1 - 2 * core
    targets = {
        TO_LOW: (d - 2, y),
        TO_HIGH: (d + 2, y),
        OWN: (partner, y),
        PASSED: (partner, y),
        TO_UNDER: (d, y - 1),
        TO_OVER: (d, y + 1),
    }
    place = lax.rem(d, ROW)
    never = d < 0
    first = (d == 0) & (y == 0)
    leads = {
        TO_LOW: never,
        TO_HIGH: first | (place >= ROW - 2),
        OWN: first,
        TO_UNDER: never,
        TO_OVER: first,
    }
    late = {
        TO_LOW: ((d == 2) & (y == 0)) | ((place < 2) & (d >= ROW)),
        TO_HIGH: never,
        OWN: (d == 1) & (y == 0),
        TO_UNDER: (d == 0) & (y == 1),
        TO_OVER: never,
    }
    meets_z = late[TO_LOW] | late[OWN]
    slow_high = (place >= ROW - 2) & has_high
    late_z = meets_z | slow_high
    early_core = jnp.where(slow_high, 1, 0)
    row = lax.div(d, ROW)
    relays = (place >= ROW - 2) & (d >= ROW)
    greets = (place < 2) & (d >= ROW)
    detours_raw = {chunks - 1: 0, chunks - 2: 1}
    detours_sum = {0: 0, 1: 2}

    def detour(r):
        return slow_high & (row >= detours_raw[r]) if r in detours_raw else never

    def relayed(r):
        return relays & (row >= detours_raw[r] + 1)

    def detour_sum(r):
        return slow_high & (row >= detours_sum[r]) if r in detours_sum else never

    def relayed_sum(r):
        return relays & (row >= detours_sum[r] + 1)

    late_y = late[TO_UNDER]
    pass_out = jnp.where(core == 0, d < energy_devices - 2, d >= 2)
    pass_in = jnp.where(core == 0, d >= 2, d < energy_devices - 2)
    slot_of = {TO_LOW: 6, TO_HIGH: 0, OWN: 2 + 2 * core, PASSED: 4 - 2 * core}
    passed_from = 6 - 6 * core
    kept_from = 6 * core

    barrier = pltpu.get_barrier_semaphore()
    count = jnp.int32(0)
    for kind in (TO_LOW, TO_HIGH, OWN, TO_UNDER, TO_OVER):
        count = count + jnp.where(exists[kind], 1, 0) - jnp.where(late[kind], 1, 0)

        @pl.when(exists[kind] & jnp.logical_not(leads[kind]))
        def _(kind=kind):
            pl.semaphore_signal(barrier, inc=1, device_id=targets[kind], device_id_type=MESH)

    def remote(source, target, send, recv, kind):
        return pltpu.make_async_remote_copy(
            src_ref=source,
            dst_ref=target,
            send_sem=send,
            recv_sem=recv,
            device_id=targets[kind] if isinstance(kind, int) else kind,
            device_id_type=MESH,
        )

    def raw_copy(kind, r):
        send, recv = sent.at[kind], raw_recv.at[kind, r]
        if kind in (TO_UNDER, TO_OVER):
            source = green.at[:, :, 1, pl.ds(r * rows, rows), :]
            side = 1 if kind == TO_UNDER else 0
            return remote(source, raw_y[r].at[side], send, recv, kind)
        target = raw_z[r].at[pl.ds(slot_of[kind], 2)]
        if kind == PASSED:
            source = raw_z[r].at[pl.ds(passed_from, 2)]
        else:
            source = green.at[:, :, 0, pl.ds(r * rows, rows), :]
        return remote(source, target, send, recv, kind)

    def sum_copy(kind, a, r):
        index = a * chunks + r
        send, recv = sent.at[kind], sum_recv.at[kind, index]
        if kind in (TO_UNDER, TO_OVER):
            side = 1 if kind == TO_UNDER else 0
            return remote(
                sent_y[a][r].at[1 - side], summed_y[a][r].at[side], send, recv, kind
            )
        target = summed_z[a][r].at[pl.ds(slot_of[kind], 2)]
        if kind == PASSED:
            source = summed_z[a][r].at[pl.ds(passed_from, 2)]
        else:
            source = own_sum[a][r]
        return remote(source, target, send, recv, kind)

    def raw_detour(r):
        source = green.at[:, :, 0, pl.ds(r * rows, rows), :]
        send = sent.at[TO_HIGH]
        return remote(source, relay_raw[r], send, relay_recv.at[chunks - 1 - r], (d + ROW, y))

    def sum_detour(a, r):
        index = a * chunks + r
        send, recv = sent.at[TO_HIGH], relay_recv.at[2 + 2 * a + r]
        return remote(own_sum[a][r], relay_sum[a][r], send, recv, (d + ROW, y))

    def raw_relay(r):
        target, recv = raw_z[r].at[0:2], raw_recv.at[TO_HIGH, r]
        return remote(relay_raw[r], target, relay_send.at[chunks - 1 - r], recv, (d - ROW + 2, y))

    def sum_relay(a, r):
        index = a * chunks + r
        send, recv = relay_send.at[2 + 2 * a + r], sum_recv.at[TO_HIGH, index]
        return remote(relay_sum[a][r], summed_z[a][r].at[0:2], send, recv, (d - ROW + 2, y))

    def relay_raw_step(r, condition):
        @pl.when(condition)
        def _():
            raw_detour(r).wait_recv()
            raw_relay(r).start()

    def relay_step(at):
        if at == 0:
            relay_raw_step(chunks - 2, relays & (row >= 2))
            relay_raw_step(chunks - 1, relays & (row == 1))
        if at == 1:
            relay_raw_step(chunks - 1, relays & (row >= 2))
        if at - 2 in detours_sum:
            r = at - 2

            @pl.when(relayed_sum(r))
            def _():
                for a in range(2):
                    sum_detour(a, r).wait_recv()
                    sum_relay(a, r).start()

    def raw_arrival(r, start, which):
        place = raw_z[r].at[pl.ds(start, 2)]
        return remote(place, place, sent.at[which], raw_recv.at[which, r], OWN)

    def sum_arrival(a, r, start, which):
        place, index = summed_z[a][r].at[pl.ds(start, 2)], a * chunks + r
        return remote(place, place, sent.at[which], sum_recv.at[which, index], OWN)

    locals_ = [
        pltpu.make_async_copy(source, target, local_sem.at[i])
        for i, (source, target) in enumerate(
            (
                (green_hbm, green),
                (coupling_hbm, coupling),
                (up_hbm, up),
                (down_hbm, down),
                (up_weight_hbm, up_weight),
                (down_weight_hbm, down_weight),
                (neighbours_hbm, neighbours),
                (strength_hbm, strength),
            )
        )
    ]
    for copy in locals_:
        copy.start()

    @pl.when(greets)
    def _():
        pl.semaphore_signal(barrier, inc=1, device_id=(d + ROW - 2, y), device_id_type=MESH)

    @pl.when(relays)
    def _():
        pl.semaphore_signal(barrier, inc=1, device_id=(d - ROW, y), device_id_type=MESH)

    count = count + jnp.where(relays, 1, 0) + jnp.where(slow_high, 1, 0)
    with scope("S_barrier"):
        pl.semaphore_wait(barrier, count)

    for kind in (TO_HIGH, OWN, TO_OVER):

        @pl.when(exists[kind] & leads[kind])
        def _(kind=kind):
            pl.semaphore_signal(ready, inc=1, device_id=targets[kind], device_id_type=MESH)

    locals_[0].wait()
    for kind in (TO_LOW, TO_HIGH, TO_UNDER, TO_OVER, OWN):

        @pl.when(exists[kind] & jnp.logical_not(late[kind]))
        def _(kind=kind):
            for r in range(chunks):
                if kind != TO_HIGH or r not in detours_raw:
                    raw_copy(kind, r).start()
                    continue

                @pl.when(detour(r))
                def _(r=r):
                    raw_detour(r).start()

                @pl.when(jnp.logical_not(detour(r)))
                def _(r=r):
                    raw_copy(TO_HIGH, r).start()

    def clear(condition, refs):
        @pl.when(jnp.logical_not(condition))
        def _():
            for ref in refs:
                ref[...] = jnp.zeros(ref.shape, ref.dtype)

    flat_z = [ref for a in range(2) for ref in summed_z[a]]
    flat_y = [ref for a in range(2) for ref in summed_y[a]]
    clear(has_low, [ref.at[0:2] for ref in raw_z + flat_z])
    clear(has_high, [ref.at[6:8] for ref in raw_z + flat_z])
    clear(has_under, [ref.at[0] for ref in raw_y + flat_y])
    clear(has_over, [ref.at[1] for ref in raw_y + flat_y])

    with scope("S_localwait"):
        for copy in locals_[1:]:
            copy.wait()

    clusters = 2 * atom_devices
    first_energy = 2 * d
    first_cluster = 2 * y

    def table(a, b):
        row = lax.rem(a + clusters, clusters)
        inside = (a >= 0) & (a < clusters) & (b >= 0) & (b < clusters)
        total = jnp.float32(0.0)
        for j in range(neighbours.shape[0]):
            total = total + jnp.where(neighbours[j, row] == b, strength[j, row], jnp.float32(0.0))
        return jnp.where(inside, total, jnp.float32(0.0))

    def entry(a, b):
        return table(first_cluster + a, first_cluster + b)

    reach = {
        (a, b): entry(a, b) for a in range(-2, 4) for b in range(-2, 4)
        if abs(a - b) <= 2 and (0 <= a < 2 or 0 <= b < 2)
    }

    up_slot, down_slot, up_factor, down_factor = [], [], [], []
    for e in range(2):
        u, l = up[e], down[e]
        up_slot.append(jnp.where(u >= 0, jnp.minimum(jnp.maximum(u - first_energy + 2, 4), 7), 7))
        down_slot.append(jnp.where(l >= 0, jnp.minimum(jnp.maximum(l - first_energy + 4, 0), 3), 0))
        up_factor.append(jnp.where(u >= 0, up_weight[e], jnp.float32(0.0)))
        down_factor.append(jnp.where(l >= 0, down_weight[e], jnp.float32(0.0)))

    def dot(left, right):
        return jnp.dot(left, right, preferred_element_type=F32)

    scale = 1.0 / (2.0 * orbitals)
    for a in range(2):
        turned = coupling[a].T
        for e in range(2):
            for part in range(2):
                x = dot(turned, green[e, a, part]) * scale
                x_big[a, e, 0:orbitals, part * orbitals : (part + 1) * orbitals] = x.astype(BF16)
                other = -x if part == 1 else x
                x_big[a, e, orbitals:, (1 - part) * orbitals : (2 - part) * orbitals] = other.astype(BF16)
                gc[a, e, :, part * orbitals : (part + 1) * orbitals] = dot(
                    green[e, a, part], coupling[a]
                ).astype(BF16)

    def wide(value):
        return value.astype(F32)

    def cluster_sums(r):
        span = pl.ds(r * rows, rows)
        for e in range(2):
            terms = {
                -2: wide(raw_y[r][0, e, 0]),
                -1: wide(raw_y[r][0, e, 1]),
                0: wide(green[e, 0, 1, span, :]),
                1: wide(green[e, 1, 1, span, :]),
                2: wide(raw_y[r][1, e, 0]),
                3: wide(raw_y[r][1, e, 1]),
            }
            for a in range(2):
                total = None
                for b in range(a - 2, a + 3):
                    piece = reach[a, b] * terms[b]
                    total = piece if total is None else total + piece
                own_sum[a][r][e] = total.astype(BF16)

    def energy_sums(r):
        for e in range(2):
            values = []
            for c in range(2):
                value = (
                    up_factor[e] * wide(raw_z[r][up_slot[e], c])
                    + down_factor[e] * wide(raw_z[r][down_slot[e], c])
                ).astype(BF16)
                hidden[r][e, c] = value
                values.append(wide(value))
            sent_y[0][r][0, e] = (reach[-2, 0] * values[0]).astype(BF16)
            sent_y[1][r][0, e] = (reach[-1, 0] * values[0] + reach[-1, 1] * values[1]).astype(BF16)
            sent_y[0][r][1, e] = (reach[2, 0] * values[0] + reach[2, 1] * values[1]).astype(BF16)
            sent_y[1][r][1, e] = (reach[3, 1] * values[1]).astype(BF16)

    def start_sums(kinds, a, r, only=None):
        for kind in kinds:
            condition = exists[kind]
            if only is not None:
                condition = late[kind] if only else condition & jnp.logical_not(late[kind])
            if kind == TO_HIGH and r in detours_sum and only is not True:
                condition = condition & jnp.logical_not(detour_sum(r))

            @pl.when(condition)
            def _(kind=kind):
                sum_copy(kind, a, r).start()

    def pass_raw(r, whose=None):
        @pl.when(pass_out if whose is None else pass_out & (core == whose))
        def _():
            with scope(f"W_zraw{r}"):
                raw_arrival(r, passed_from, core).wait_recv()
            raw_copy(PASSED, r).start()

    def over_energies(r, only=None):
        with scope(f"W_own{r}"):
            raw_copy(OWN, r).wait_recv()

        @pl.when(pass_in)
        def _():
            with scope(f"W_pass{r}"):
                raw_arrival(r, kept_from, 1 - core).wait_recv()
                raw_copy(PASSED, r).wait_recv()

        energy_sums(r)
        start_sums(OVER_Y, 0, r, only)

    def over_clusters(r, only=None):
        with scope(f"W_yraw{r}"):

            @pl.when(has_over)
            def _():
                raw_copy(TO_UNDER, r).wait_recv()

            @pl.when(has_under)
            def _():
                raw_copy(TO_OVER, r).wait_recv()

        cluster_sums(r)
        start_sums(OVER_Z, 0, r, only)

    def meet(kinds):
        pl.semaphore_wait(ready, 1)
        for kind in kinds:

            @pl.when(late[kind])
            def _(kind=kind):
                for r in range(chunks):
                    raw_copy(kind, r).start()

    @pl.when(jnp.logical_not(late_y | late_z))
    def _():
        for r in range(chunks):
            pass_raw(r)
            if r:
                over_energies(r - 1)
            over_clusters(r)
            relay_step(r)
        for r in range(chunks):
            start_sums(OVER_Z, 1, r)
        start_sums(OVER_Y, 1, 0)
        over_energies(chunks - 1)
        for r in range(1, chunks):
            start_sums(OVER_Y, 1, r)

    @pl.when(late_y)
    def _():
        for r in range(chunks):
            pass_raw(r)
            if r:
                over_energies(r - 1, False)
                if r == 1:
                    meet(OVER_Y)
                start_sums(OVER_Y, 0, r - 1, True)
        start_sums(OVER_Y, 1, 0)
        over_energies(chunks - 1)
        for r in range(1, chunks):
            start_sums(OVER_Y, 1, r)
        for r in range(chunks):
            over_clusters(r)
        for r in range(chunks):
            start_sums(OVER_Z, 1, r)

    @pl.when(late_z)
    def _():
        for r in range(chunks):
            pass_raw(r, early_core)
            over_clusters(r, False)
            if r == 0:

                @pl.when(meets_z)
                def _():
                    meet(OVER_Z)

            if r in detours_sum:

                @pl.when(detour_sum(r))
                def _(r=r):
                    for a in range(2):
                        sum_detour(a, r).start()

            start_sums(OVER_Z, 0, r, True)
            start_sums(OVER_Z, 1, r)
            relay_step(r)
        for r in range(chunks):
            pass_raw(r, 1 - early_core)
            if r:
                over_energies(r - 1)
        start_sums(OVER_Y, 1, 0)
        over_energies(chunks - 1)
        for r in range(1, chunks):
            start_sums(OVER_Y, 1, r)

    def read(a, r):
        span = pl.ds(r * rows, rows)
        with scope(f"W_ysum{a}{r}"):

            @pl.when(has_over)
            def _():
                sum_copy(TO_UNDER, a, r).wait_recv()

            @pl.when(has_under)
            def _():
                sum_copy(TO_OVER, a, r).wait_recv()

        for e in range(2):
            total = wide(summed_y[a][r][0, e]) + wide(summed_y[a][r][1, e])
            for c in range(2):
                total = total + reach[a, c] * wide(hidden[r][e, c])
            reader[a, e, :, 0:orbitals] = total.astype(BF16)
        with scope(f"W_zpass{a}{r}"):
            sum_copy(OWN, a, r).wait_recv()

            @pl.when(pass_in)
            def _():
                sum_arrival(a, r, kept_from, 1 - core).wait_recv()
                sum_copy(PASSED, a, r).wait_recv()

        for e in range(2):
            total = up_factor[e] * wide(summed_z[a][r][up_slot[e]]) + down_factor[e] * wide(
                summed_z[a][r][down_slot[e]]
            )
            reader[a, e, :, orbitals:] = total.astype(BF16)
        for e in range(2):
            value = dot(reader[a, e], x_big[a, e])
            real, imag = value[:, :orbitals].astype(BF16), value[:, orbitals:].astype(BF16)
            after = pl.ds(orbitals + r * rows, rows)
            y_big[a, e, span, 0:orbitals] = real
            y_big[a, e, span, orbitals:] = imag
            y_big[a, e, after, 0:orbitals] = -imag
            y_big[a, e, after, orbitals:] = real

    def finish(a):
        for e in range(2):
            first = dot(coupling[a], y_big[a, e, 0:orbitals])
            real, imag = first[:, :orbitals].astype(BF16), first[:, orbitals:].astype(BF16)
            f_big[e, 0:orbitals, 0:orbitals] = real
            f_big[e, 0:orbitals, orbitals:] = imag
            f_big[e, orbitals:, 0:orbitals] = -imag
            f_big[e, orbitals:, orbitals:] = real
        for e in range(2):
            second_cat[e] = dot(gc[a, e], y_big[a, e])
        for e in range(2):
            third = dot(second_cat[e].astype(BF16), f_big[e])
            for part in range(2):
                side = slice(part * orbitals, (part + 1) * orbitals)
                out_ref[e, a, part] = (
                    wide(green[e, a, part]) + second_cat[e, :, side] + third[:, side]
                ).astype(BF16)

    def pass_sum(a, r, condition):
        @pl.when(condition)
        def _():
            with scope(f"W_zsum{a}{r}"):
                sum_arrival(a, r, passed_from, core).wait_recv()
            sum_copy(PASSED, a, r).start()

    steps = [(a, r) for a in range(2) for r in range(chunks)]
    for at, (a, r) in enumerate(steps):
        pass_sum(a, r, pass_out if at <= chunks else pass_out & jnp.logical_not(greets))
        if at == chunks:
            for ahead in range(1, chunks - 1):
                pass_sum(1, ahead, pass_out & greets)
        if at == chunks + 1:
            pass_sum(1, chunks - 1, pass_out & greets)
        if at:
            read(*steps[at - 1])
            if steps[at - 1][1] == chunks - 1:
                finish(steps[at - 1][0])
    read(*steps[-1])
    with scope("S_finish1"):
        finish(1)

    with scope("S_sends"):
        for kind in range(6):

            @pl.when(pass_out if kind == PASSED else exists[kind])
            def _(kind=kind):
                remote(green, green, sent.at[kind], raw_recv.at[kind, 0], OWN).wait_send()

        for r in detours_raw:

            @pl.when(relayed(r))
            def _(r=r):
                raw_relay(r).wait_send()

        for r in detours_sum:

            @pl.when(relayed_sum(r))
            def _(r=r):
                for a in range(2):
                    sum_relay(a, r).wait_send()


def solution(mesh):
    energy_devices, atom_devices = mesh.shape["energy"], mesh.shape["atom"]

    def on_device(
        green_blocks, coupling, up_partner, down_partner, up_weight, down_weight, neighbours, strength
    ):
        orbitals = green_blocks.shape[-1]
        rows = orbitals // CHUNKS
        slots = neighbours.shape[1]
        clusters = neighbours.shape[0]

        def vmem(*shape, dtype=BF16):
            return pltpu.VMEM(shape, dtype)

        many = range(CHUNKS)
        scratch = (
            [vmem(8, 2, rows, orbitals) for _ in many]
            + [vmem(2, 2, 2, rows, orbitals) for _ in many]
            + [vmem(8, rows, orbitals) for _ in range(2 * CHUNKS)]
            + [vmem(2, 2, rows, orbitals) for _ in range(2 * CHUNKS)]
            + [vmem(2, rows, orbitals) for _ in range(2 * CHUNKS)]
            + [vmem(2, 2, rows, orbitals) for _ in many]
            + [vmem(2, 2, rows, orbitals) for _ in range(2)]
            + [vmem(2, rows, orbitals) for _ in range(4)]
            + [vmem(2, 2, rows, orbitals) for _ in range(2 * CHUNKS)]
            + [
                vmem(2, 2, 2, orbitals, orbitals),
                vmem(2, orbitals, orbitals),
                pltpu.SMEM((2,), jnp.int32),
                pltpu.SMEM((2,), jnp.int32),
                pltpu.SMEM((2,), F32),
                pltpu.SMEM((2,), F32),
                pltpu.SMEM((slots, clusters), jnp.int32),
                pltpu.SMEM((slots, clusters), F32),
                vmem(2, 2, rows, 2 * orbitals),
                vmem(2, 2, 2 * orbitals, 2 * orbitals),
                vmem(2, 2, orbitals, 2 * orbitals),
                vmem(2, 2, 2 * orbitals, 2 * orbitals),
                vmem(2, 2 * orbitals, 2 * orbitals),
                vmem(2, orbitals, 2 * orbitals, dtype=F32),
                pltpu.SemaphoreType.DMA((6,)),
                pltpu.SemaphoreType.DMA((6, CHUNKS)),
                pltpu.SemaphoreType.DMA((6, 2 * CHUNKS)),
                pltpu.SemaphoreType.DMA((6,)),
                pltpu.SemaphoreType.DMA((6,)),
                pltpu.SemaphoreType.DMA((8,)),
                pltpu.SemaphoreType.REGULAR,
            ]
        )
        return pl.pallas_call(
            functools.partial(kernel, energy_devices, atom_devices),
            out_shape=jax.ShapeDtypeStruct(green_blocks.shape, green_blocks.dtype),
            in_specs=[pl.BlockSpec(memory_space=pl.ANY)] * 8,
            out_specs=pl.BlockSpec(memory_space=pltpu.VMEM),
            scratch_shapes=scratch,
            compiler_params=pltpu.CompilerParams(
                collective_id=0, has_side_effects=True, vmem_limit_bytes=24 * 1024 * 1024
            ),
            name="update",
        )(
            *(
                pltpu.with_memory_space_constraint(array, pltpu.HBM)
                for array in (
                    green_blocks,
                    coupling,
                    up_partner,
                    down_partner,
                    up_weight,
                    down_weight,
                    neighbours.T,
                    strength.T,
                )
            )
        )

    in_specs = (
        P("energy", "atom", None, None, None),
        P("atom", None, None),
        P("energy"),
        P("energy"),
        P("energy"),
        P("energy"),
        P(),
        P(),
    )
    out_specs = P("energy", "atom", None, None, None)
    return jax.shard_map(
        on_device, mesh=mesh, in_specs=in_specs, out_specs=out_specs, check_vma=False
    )
```

```python
import functools

import jax
import jax.numpy as jnp
from jax import lax
from jax.experimental import pallas as pl
from jax.experimental.pallas import tpu as pltpu
from jax.sharding import PartitionSpec as P

MESH = pl.DeviceIdType.MESH
CHUNKS = 4
ROW = 24
F32 = jnp.float32
BF16 = jnp.bfloat16

TO_LOW, TO_HIGH, OWN, PASSED, TO_UNDER, TO_OVER = range(6)
OVER_Z = (TO_LOW, TO_HIGH, OWN)
OVER_Y = (TO_UNDER, TO_OVER)
scope = jax.named_scope


def kernel(
    energy_devices,
    atom_devices,
    green_hbm,
    coupling_hbm,
    up_hbm,
    down_hbm,
    up_weight_hbm,
    down_weight_hbm,
    neighbours_hbm,
    strength_hbm,
    out_ref,
    *scratch,
):
    chunks = CHUNKS
    orbitals = green_hbm.shape[-1]
    rows = orbitals // chunks
    names = iter(scratch)

    def take(count):
        return [next(names) for _ in range(count)]

    raw_z = take(chunks)
    raw_y = take(chunks)
    summed_z = [take(chunks) for _ in range(2)]
    summed_y = [take(chunks) for _ in range(2)]
    own_sum = [take(chunks) for _ in range(2)]
    hidden = take(chunks)
    relay_raw = dict(zip((chunks - 2, chunks - 1), take(2)))
    relay_sum = [take(2) for _ in range(2)]
    sent_y = [take(chunks) for _ in range(2)]
    (
        green,
        coupling,
        up,
        down,
        up_weight,
        down_weight,
        neighbours,
        strength,
        reader,
        x_big,
        gc,
        y_big,
        f_big,
        second_cat,
        sent,
        raw_recv,
        sum_recv,
        relay_send,
        relay_recv,
        local_sem,
        ready,
    ) = names

    d = lax.axis_index("energy")
    y = lax.axis_index("atom")
    core = lax.rem(d, 2)
    has_low, has_high = d >= 2, d < energy_devices - 2
    has_under, has_over = y >= 1, y < atom_devices - 1
    exists = {
        TO_LOW: has_low,
        TO_HIGH: has_high,
        OWN: d >= 0,
        TO_UNDER: has_under,
        TO_OVER: has_over,
    }
    partner = d + 1 - 2 * core
    targets = {
        TO_LOW: (d - 2, y),
        TO_HIGH: (d + 2, y),
        OWN: (partner, y),
        PASSED: (partner, y),
        TO_UNDER: (d, y - 1),
        TO_OVER: (d, y + 1),
    }
    place = lax.rem(d, ROW)
    never = d < 0
    first = (d == 0) & (y == 0)
    leads = {
        TO_LOW: never,
        TO_HIGH: first | (place >= ROW - 2),
        OWN: first,
        TO_UNDER: never,
        TO_OVER: first,
    }
    late = {
        TO_LOW: ((d == 2) & (y == 0)) | ((place < 2) & (d >= ROW)),
        TO_HIGH: never,
        OWN: (d == 1) & (y == 0),
        TO_UNDER: (d == 0) & (y == 1),
        TO_OVER: never,
    }
    meets_z = late[TO_LOW] | late[OWN]
    slow_high = (place >= ROW - 2) & has_high
    late_z = meets_z | slow_high
    early_core = jnp.where(slow_high, 1, 0)
    row = lax.div(d, ROW)
    relays = (place >= ROW - 2) & (d >= ROW)
    greets = (place < 2) & (d >= ROW)
    detours_raw = {chunks - 1: 0, chunks - 2: 1}
    detours_sum = {0: 0, 1: 2}

    def detour(r):
        return slow_high & (row >= detours_raw[r]) if r in detours_raw else never

    def relayed(r):
        return relays & (row >= detours_raw[r] + 1)

    def detour_sum(r):
        return slow_high & (row >= detours_sum[r]) if r in detours_sum else never

    def relayed_sum(r):
        return relays & (row >= detours_sum[r] + 1)

    late_y = late[TO_UNDER]
    pass_out = jnp.where(core == 0, d < energy_devices - 2, d >= 2)
    pass_in = jnp.where(core == 0, d >= 2, d < energy_devices - 2)
    slot_of = {TO_LOW: 6, TO_HIGH: 0, OWN: 2 + 2 * core, PASSED: 4 - 2 * core}
    passed_from = 6 - 6 * core
    kept_from = 6 * core

    barrier = pltpu.get_barrier_semaphore()
    count = jnp.int32(0)
    for kind in (TO_LOW, TO_HIGH, OWN, TO_UNDER, TO_OVER):
        count = count + jnp.where(exists[kind], 1, 0) - jnp.where(late[kind], 1, 0)

        @pl.when(exists[kind] & jnp.logical_not(leads[kind]))
        def _(kind=kind):
            pl.semaphore_signal(barrier, inc=1, device_id=targets[kind], device_id_type=MESH)

    def remote(source, target, send, recv, kind):
        return pltpu.make_async_remote_copy(
            src_ref=source,
            dst_ref=target,
            send_sem=send,
            recv_sem=recv,
            device_id=targets[kind] if isinstance(kind, int) else kind,
            device_id_type=MESH,
        )

    def raw_copy(kind, r):
        send, recv = sent.at[kind], raw_recv.at[kind, r]
        if kind in (TO_UNDER, TO_OVER):
            source = green.at[:, :, 1, pl.ds(r * rows, rows), :]
            side = 1 if kind == TO_UNDER else 0
            return remote(source, raw_y[r].at[side], send, recv, kind)
        target = raw_z[r].at[pl.ds(slot_of[kind], 2)]
        if kind == PASSED:
            source = raw_z[r].at[pl.ds(passed_from, 2)]
        else:
            source = green.at[:, :, 0, pl.ds(r * rows, rows), :]
        return remote(source, target, send, recv, kind)

    def sum_copy(kind, a, r):
        index = a * chunks + r
        send, recv = sent.at[kind], sum_recv.at[kind, index]
        if kind in (TO_UNDER, TO_OVER):
            side = 1 if kind == TO_UNDER else 0
            return remote(
                sent_y[a][r].at[1 - side], summed_y[a][r].at[side], send, recv, kind
            )
        target = summed_z[a][r].at[pl.ds(slot_of[kind], 2)]
        if kind == PASSED:
            source = summed_z[a][r].at[pl.ds(passed_from, 2)]
        else:
            source = own_sum[a][r]
        return remote(source, target, send, recv, kind)

    def raw_detour(r):
        source = green.at[:, :, 0, pl.ds(r * rows, rows), :]
        send = sent.at[TO_HIGH]
        return remote(source, relay_raw[r], send, relay_recv.at[chunks - 1 - r], (d + ROW, y))

    def sum_detour(a, r):
        index = a * chunks + r
        send, recv = sent.at[TO_HIGH], relay_recv.at[2 + 2 * a + r]
        return remote(own_sum[a][r], relay_sum[a][r], send, recv, (d + ROW, y))

    def raw_relay(r):
        target, recv = raw_z[r].at[0:2], raw_recv.at[TO_HIGH, r]
        return remote(relay_raw[r], target, relay_send.at[chunks - 1 - r], recv, (d - ROW + 2, y))

    def sum_relay(a, r):
        index = a * chunks + r
        send, recv = relay_send.at[2 + 2 * a + r], sum_recv.at[TO_HIGH, index]
        return remote(relay_sum[a][r], summed_z[a][r].at[0:2], send, recv, (d - ROW + 2, y))

    def relay_raw_step(r, condition):
        @pl.when(condition)
        def _():
            raw_detour(r).wait_recv()
            raw_relay(r).start()

    def relay_step(at):
        if at == 0:
            relay_raw_step(chunks - 2, relays & (row >= 2))
            relay_raw_step(chunks - 1, relays & (row == 1))
        if at == 1:
            relay_raw_step(chunks - 1, relays & (row >= 2))
        if at - 2 in detours_sum:
            r = at - 2

            @pl.when(relayed_sum(r))
            def _():
                for a in range(2):
                    sum_detour(a, r).wait_recv()
                    sum_relay(a, r).start()

    def raw_arrival(r, start, which):
        place = raw_z[r].at[pl.ds(start, 2)]
        return remote(place, place, sent.at[which], raw_recv.at[which, r], OWN)

    def sum_arrival(a, r, start, which):
        place, index = summed_z[a][r].at[pl.ds(start, 2)], a * chunks + r
        return remote(place, place, sent.at[which], sum_recv.at[which, index], OWN)

    locals_ = [
        pltpu.make_async_copy(source, target, local_sem.at[i])
        for i, (source, target) in enumerate(
            (
                (green_hbm, green),
                (coupling_hbm, coupling),
                (up_hbm, up),
                (down_hbm, down),
                (up_weight_hbm, up_weight),
                (down_weight_hbm, down_weight),
                (neighbours_hbm, neighbours),
                (strength_hbm, strength),
            )
        )
    ]
    for copy in locals_:
        copy.start()

    @pl.when(greets)
    def _():
        pl.semaphore_signal(barrier, inc=1, device_id=(d + ROW - 2, y), device_id_type=MESH)

    @pl.when(relays)
    def _():
        pl.semaphore_signal(barrier, inc=1, device_id=(d - ROW, y), device_id_type=MESH)

    count = count + jnp.where(relays, 1, 0) + jnp.where(slow_high, 1, 0)
    with scope("S_barrier"):
        pl.semaphore_wait(barrier, count)

    for kind in (TO_HIGH, OWN, TO_OVER):

        @pl.when(exists[kind] & leads[kind])
        def _(kind=kind):
            pl.semaphore_signal(ready, inc=1, device_id=targets[kind], device_id_type=MESH)

    locals_[0].wait()
    for kind in (TO_LOW, TO_HIGH, TO_UNDER, TO_OVER, OWN):

        @pl.when(exists[kind] & jnp.logical_not(late[kind]))
        def _(kind=kind):
            for r in range(chunks):
                if kind != TO_HIGH or r not in detours_raw:
                    raw_copy(kind, r).start()
                    continue

                @pl.when(detour(r))
                def _(r=r):
                    raw_detour(r).start()

                @pl.when(jnp.logical_not(detour(r)))
                def _(r=r):
                    raw_copy(TO_HIGH, r).start()

    def clear(condition, refs):
        @pl.when(jnp.logical_not(condition))
        def _():
            for ref in refs:
                ref[...] = jnp.zeros(ref.shape, ref.dtype)

    flat_z = [ref for a in range(2) for ref in summed_z[a]]
    flat_y = [ref for a in range(2) for ref in summed_y[a]]
    clear(has_low, [ref.at[0:2] for ref in raw_z + flat_z])
    clear(has_high, [ref.at[6:8] for ref in raw_z + flat_z])
    clear(has_under, [ref.at[0] for ref in raw_y + flat_y])
    clear(has_over, [ref.at[1] for ref in raw_y + flat_y])

    with scope("S_localwait"):
        for copy in locals_[1:]:
            copy.wait()

    clusters = 2 * atom_devices
    first_energy = 2 * d
    first_cluster = 2 * y

    def table(a, b):
        row = lax.rem(a + clusters, clusters)
        inside = (a >= 0) & (a < clusters) & (b >= 0) & (b < clusters)
        total = jnp.float32(0.0)
        for j in range(neighbours.shape[0]):
            total = total + jnp.where(neighbours[j, row] == b, strength[j, row], jnp.float32(0.0))
        return jnp.where(inside, total, jnp.float32(0.0))

    def entry(a, b):
        return table(first_cluster + a, first_cluster + b)

    reach = {
        (a, b): entry(a, b) for a in range(-2, 4) for b in range(-2, 4)
        if abs(a - b) <= 2 and (0 <= a < 2 or 0 <= b < 2)
    }

    up_slot, down_slot, up_factor, down_factor = [], [], [], []
    for e in range(2):
        u, l = up[e], down[e]
        up_slot.append(jnp.where(u >= 0, jnp.minimum(jnp.maximum(u - first_energy + 2, 4), 7), 7))
        down_slot.append(jnp.where(l >= 0, jnp.minimum(jnp.maximum(l - first_energy + 4, 0), 3), 0))
        up_factor.append(jnp.where(u >= 0, up_weight[e], jnp.float32(0.0)))
        down_factor.append(jnp.where(l >= 0, down_weight[e], jnp.float32(0.0)))

    def dot(left, right):
        return jnp.dot(left, right, preferred_element_type=F32)

    scale = 1.0 / (2.0 * orbitals)
    for a in range(2):
        turned = coupling[a].T
        for e in range(2):
            for part in range(2):
                x = dot(turned, green[e, a, part]) * scale
                x_big[a, e, 0:orbitals, part * orbitals : (part + 1) * orbitals] = x.astype(BF16)
                other = -x if part == 1 else x
                x_big[a, e, orbitals:, (1 - part) * orbitals : (2 - part) * orbitals] = other.astype(BF16)
                gc[a, e, :, part * orbitals : (part + 1) * orbitals] = dot(
                    green[e, a, part], coupling[a]
                ).astype(BF16)

    def wide(value):
        return value.astype(F32)

    def cluster_sums(r):
        span = pl.ds(r * rows, rows)
        for e in range(2):
            terms = {
                -2: wide(raw_y[r][0, e, 0]),
                -1: wide(raw_y[r][0, e, 1]),
                0: wide(green[e, 0, 1, span, :]),
                1: wide(green[e, 1, 1, span, :]),
                2: wide(raw_y[r][1, e, 0]),
                3: wide(raw_y[r][1, e, 1]),
            }
            for a in range(2):
                total = None
                for b in range(a - 2, a + 3):
                    piece = reach[a, b] * terms[b]
                    total = piece if total is None else total + piece
                own_sum[a][r][e] = total.astype(BF16)

    def energy_sums(r):
        for e in range(2):
            values = []
            for c in range(2):
                value = (
                    up_factor[e] * wide(raw_z[r][up_slot[e], c])
                    + down_factor[e] * wide(raw_z[r][down_slot[e], c])
                ).astype(BF16)
                hidden[r][e, c] = value
                values.append(wide(value))
            sent_y[0][r][0, e] = (reach[-2, 0] * values[0]).astype(BF16)
            sent_y[1][r][0, e] = (reach[-1, 0] * values[0] + reach[-1, 1] * values[1]).astype(BF16)
            sent_y[0][r][1, e] = (reach[2, 0] * values[0] + reach[2, 1] * values[1]).astype(BF16)
            sent_y[1][r][1, e] = (reach[3, 1] * values[1]).astype(BF16)

    def start_sums(kinds, a, r, only=None, extra=None):
        for kind in kinds:
            condition = exists[kind] if extra is None else exists[kind] & extra
            if only is not None:
                condition = late[kind] if only else condition & jnp.logical_not(late[kind])
            if kind == TO_HIGH and r in detours_sum and only is not True:
                condition = condition & jnp.logical_not(detour_sum(r))

            @pl.when(condition)
            def _(kind=kind):
                sum_copy(kind, a, r).start()

    def pass_raw(r, whose=None):
        @pl.when(pass_out if whose is None else pass_out & (core == whose))
        def _():
            with scope(f"W_zraw{r}"):
                raw_arrival(r, passed_from, core).wait_recv()
            raw_copy(PASSED, r).start()

    def over_energies(r, only=None):
        with scope(f"W_own{r}"):
            raw_copy(OWN, r).wait_recv()

        @pl.when(pass_in)
        def _():
            with scope(f"W_pass{r}"):
                raw_arrival(r, kept_from, 1 - core).wait_recv()
                raw_copy(PASSED, r).wait_recv()

        energy_sums(r)
        start_sums(OVER_Y, 0, r, only)

    def over_clusters(r, only=None):
        with scope(f"W_yraw{r}"):

            @pl.when(has_over)
            def _():
                raw_copy(TO_UNDER, r).wait_recv()

            @pl.when(has_under)
            def _():
                raw_copy(TO_OVER, r).wait_recv()

        cluster_sums(r)
        start_sums(OVER_Z, 0, r, only)

    def meet(kinds):
        pl.semaphore_wait(ready, 1)
        for kind in kinds:

            @pl.when(late[kind])
            def _(kind=kind):
                for r in range(chunks):
                    raw_copy(kind, r).start()

    @pl.when(jnp.logical_not(late_y | late_z))
    def _():
        for r in range(chunks):
            pass_raw(r)
            if r:
                over_energies(r - 1)
            over_clusters(r)
            relay_step(r)
        for r in range(chunks):
            start_sums(OVER_Z, 1, r)
        start_sums(OVER_Y, 1, 0)
        over_energies(chunks - 1)
        for r in range(1, chunks):
            start_sums(OVER_Y, 1, r)

    @pl.when(late_y)
    def _():
        for r in range(chunks):
            pass_raw(r)
            if r:
                over_energies(r - 1, False)
                if r == 1:
                    meet(OVER_Y)
                start_sums(OVER_Y, 0, r - 1, True)
        start_sums(OVER_Y, 1, 0)
        over_energies(chunks - 1)
        for r in range(1, chunks):
            start_sums(OVER_Y, 1, r)
        for r in range(chunks):
            over_clusters(r)
        for r in range(chunks):
            start_sums(OVER_Z, 1, r)

    @pl.when(late_z)
    def _():
        for r in range(chunks):
            pass_raw(r, early_core)
            over_clusters(r, False)
            if r == 0:

                @pl.when(meets_z)
                def _():
                    meet(OVER_Z)

            if r in detours_sum:

                @pl.when(detour_sum(r))
                def _(r=r):
                    for a in range(2):
                        sum_detour(a, r).start()

            start_sums(OVER_Z, 0, r, True)
            start_sums(OVER_Z, 1, r)
            relay_step(r)
        for r in range(chunks):
            pass_raw(r, 1 - early_core)
            if r:
                over_energies(r - 1)
                start_sums(OVER_Y, 1, r - 1, extra=greets)
        others = jnp.logical_not(greets)
        start_sums(OVER_Y, 1, 0, extra=others)
        over_energies(chunks - 1)
        for r in range(1, chunks - 1):
            start_sums(OVER_Y, 1, r, extra=others)
        start_sums(OVER_Y, 1, chunks - 1)

    def read(a, r):
        span = pl.ds(r * rows, rows)
        with scope(f"W_ysum{a}{r}"):

            @pl.when(has_over)
            def _():
                sum_copy(TO_UNDER, a, r).wait_recv()

            @pl.when(has_under)
            def _():
                sum_copy(TO_OVER, a, r).wait_recv()

        for e in range(2):
            total = wide(summed_y[a][r][0, e]) + wide(summed_y[a][r][1, e])
            for c in range(2):
                total = total + reach[a, c] * wide(hidden[r][e, c])
            reader[a, e, :, 0:orbitals] = total.astype(BF16)
        with scope(f"W_zpass{a}{r}"):
            sum_copy(OWN, a, r).wait_recv()

            @pl.when(pass_in)
            def _():
                sum_arrival(a, r, kept_from, 1 - core).wait_recv()
                sum_copy(PASSED, a, r).wait_recv()

        for e in range(2):
            total = up_factor[e] * wide(summed_z[a][r][up_slot[e]]) + down_factor[e] * wide(
                summed_z[a][r][down_slot[e]]
            )
            reader[a, e, :, orbitals:] = total.astype(BF16)
        for e in range(2):
            value = dot(reader[a, e], x_big[a, e])
            real, imag = value[:, :orbitals].astype(BF16), value[:, orbitals:].astype(BF16)
            after = pl.ds(orbitals + r * rows, rows)
            y_big[a, e, span, 0:orbitals] = real
            y_big[a, e, span, orbitals:] = imag
            y_big[a, e, after, 0:orbitals] = -imag
            y_big[a, e, after, orbitals:] = real

    def finish(a):
        for e in range(2):
            first = dot(coupling[a], y_big[a, e, 0:orbitals])
            real, imag = first[:, :orbitals].astype(BF16), first[:, orbitals:].astype(BF16)
            f_big[e, 0:orbitals, 0:orbitals] = real
            f_big[e, 0:orbitals, orbitals:] = imag
            f_big[e, orbitals:, 0:orbitals] = -imag
            f_big[e, orbitals:, orbitals:] = real
        for e in range(2):
            second_cat[e] = dot(gc[a, e], y_big[a, e])
        for e in range(2):
            third = dot(second_cat[e].astype(BF16), f_big[e])
            for part in range(2):
                side = slice(part * orbitals, (part + 1) * orbitals)
                out_ref[e, a, part] = (
                    wide(green[e, a, part]) + second_cat[e, :, side] + third[:, side]
                ).astype(BF16)

    def pass_sum(a, r, condition):
        @pl.when(condition)
        def _():
            with scope(f"W_zsum{a}{r}"):
                sum_arrival(a, r, passed_from, core).wait_recv()
            sum_copy(PASSED, a, r).start()

    @pl.when(jnp.logical_not(greets))
    def _():
        steps = [(a, r) for a in range(2) for r in range(chunks)]
        for at, (a, r) in enumerate(steps):
            pass_sum(a, r, pass_out)
            if at:
                read(*steps[at - 1])
                if steps[at - 1][1] == chunks - 1:
                    finish(steps[at - 1][0])
        read(*steps[-1])
        finish(1)

    @pl.when(greets)
    def _():
        last = chunks - 1
        lower, upper = pass_out & (core == 0), pass_out & (core == 1)

        @pl.when(lower)
        def _():
            for a in range(2):
                for r in range(chunks):
                    sum_arrival(a, r, passed_from, core).wait_recv()
                    sum_copy(PASSED, a, r).start()

        for r in range(1, last):
            for a in range(2):
                pass_sum(a, r, upper)
            for a in range(2):
                read(a, r)
        for a in range(2):
            pass_sum(a, 0, upper)
        read(0, 0)
        pass_sum(0, last, upper)
        read(1, 0)
        pass_sum(1, last, upper)
        read(0, last)
        finish(0)
        read(1, last)
        finish(1)

    with scope("S_sends"):
        for kind in range(6):

            @pl.when(pass_out if kind == PASSED else exists[kind])
            def _(kind=kind):
                remote(green, green, sent.at[kind], raw_recv.at[kind, 0], OWN).wait_send()

        for r in detours_raw:

            @pl.when(relayed(r))
            def _(r=r):
                raw_relay(r).wait_send()

        for r in detours_sum:

            @pl.when(relayed_sum(r))
            def _(r=r):
                for a in range(2):
                    sum_relay(a, r).wait_send()


def solution(mesh):
    energy_devices, atom_devices = mesh.shape["energy"], mesh.shape["atom"]

    def on_device(
        green_blocks, coupling, up_partner, down_partner, up_weight, down_weight, neighbours, strength
    ):
        orbitals = green_blocks.shape[-1]
        rows = orbitals // CHUNKS
        slots = neighbours.shape[1]
        clusters = neighbours.shape[0]

        def vmem(*shape, dtype=BF16):
            return pltpu.VMEM(shape, dtype)

        many = range(CHUNKS)
        scratch = (
            [vmem(8, 2, rows, orbitals) for _ in many]
            + [vmem(2, 2, 2, rows, orbitals) for _ in many]
            + [vmem(8, rows, orbitals) for _ in range(2 * CHUNKS)]
            + [vmem(2, 2, rows, orbitals) for _ in range(2 * CHUNKS)]
            + [vmem(2, rows, orbitals) for _ in range(2 * CHUNKS)]
            + [vmem(2, 2, rows, orbitals) for _ in many]
            + [vmem(2, 2, rows, orbitals) for _ in range(2)]
            + [vmem(2, rows, orbitals) for _ in range(4)]
            + [vmem(2, 2, rows, orbitals) for _ in range(2 * CHUNKS)]
            + [
                vmem(2, 2, 2, orbitals, orbitals),
                vmem(2, orbitals, orbitals),
                pltpu.SMEM((2,), jnp.int32),
                pltpu.SMEM((2,), jnp.int32),
                pltpu.SMEM((2,), F32),
                pltpu.SMEM((2,), F32),
                pltpu.SMEM((slots, clusters), jnp.int32),
                pltpu.SMEM((slots, clusters), F32),
                vmem(2, 2, rows, 2 * orbitals),
                vmem(2, 2, 2 * orbitals, 2 * orbitals),
                vmem(2, 2, orbitals, 2 * orbitals),
                vmem(2, 2, 2 * orbitals, 2 * orbitals),
                vmem(2, 2 * orbitals, 2 * orbitals),
                vmem(2, orbitals, 2 * orbitals, dtype=F32),
                pltpu.SemaphoreType.DMA((6,)),
                pltpu.SemaphoreType.DMA((6, CHUNKS)),
                pltpu.SemaphoreType.DMA((6, 2 * CHUNKS)),
                pltpu.SemaphoreType.DMA((6,)),
                pltpu.SemaphoreType.DMA((6,)),
                pltpu.SemaphoreType.DMA((8,)),
                pltpu.SemaphoreType.REGULAR,
            ]
        )
        return pl.pallas_call(
            functools.partial(kernel, energy_devices, atom_devices),
            out_shape=jax.ShapeDtypeStruct(green_blocks.shape, green_blocks.dtype),
            in_specs=[pl.BlockSpec(memory_space=pl.ANY)] * 8,
            out_specs=pl.BlockSpec(memory_space=pltpu.VMEM),
            scratch_shapes=scratch,
            compiler_params=pltpu.CompilerParams(
                collective_id=0, has_side_effects=True, vmem_limit_bytes=24 * 1024 * 1024
            ),
            name="update",
        )(
            *(
                pltpu.with_memory_space_constraint(array, pltpu.HBM)
                for array in (
                    green_blocks,
                    coupling,
                    up_partner,
                    down_partner,
                    up_weight,
                    down_weight,
                    neighbours.T,
                    strength.T,
                )
            )
        )

    in_specs = (
        P("energy", "atom", None, None, None),
        P("atom", None, None),
        P("energy"),
        P("energy"),
        P("energy"),
        P("energy"),
        P(),
        P(),
    )
    out_specs = P("energy", "atom", None, None, None)
    return jax.shard_map(
        on_device, mesh=mesh, in_specs=in_specs, out_specs=out_specs, check_vma=False
    )
```

```python
import functools

import jax
import jax.numpy as jnp
from jax import lax
from jax.experimental import pallas as pl
from jax.experimental.pallas import tpu as pltpu
from jax.sharding import PartitionSpec as P

MESH = pl.DeviceIdType.MESH
CHUNKS = 4
ROW = 24
F32 = jnp.float32
BF16 = jnp.bfloat16

TO_LOW, TO_HIGH, OWN, PASSED, TO_UNDER, TO_OVER = range(6)
ARRIVAL = (0, 1, 2, 2, 3, 3)
OVER_Z = (TO_LOW, TO_HIGH, OWN)
OVER_Y = (TO_UNDER, TO_OVER)
scope = jax.named_scope


def kernel(
    energy_devices,
    atom_devices,
    green_hbm,
    coupling_hbm,
    up_hbm,
    down_hbm,
    up_weight_hbm,
    down_weight_hbm,
    neighbours_hbm,
    strength_hbm,
    out_ref,
    *scratch,
):
    chunks = CHUNKS
    orbitals = green_hbm.shape[-1]
    rows = orbitals // chunks
    names = iter(scratch)

    def take(count):
        return [next(names) for _ in range(count)]

    raw_z = take(chunks)
    raw_y = take(chunks)
    summed_z = [take(chunks) for _ in range(2)]
    summed_y = [take(chunks) for _ in range(2)]
    own_sum = [take(chunks) for _ in range(2)]
    hidden = take(chunks)
    relay_raw = dict(zip((chunks - 2, chunks - 1), take(2)))
    relay_sum = [take(2) for _ in range(2)]
    sent_y = [take(chunks) for _ in range(2)]
    (
        green,
        coupling,
        up,
        down,
        up_weight,
        down_weight,
        neighbours,
        strength,
        reader,
        x_big,
        gc,
        y_big,
        f_big,
        second_cat,
        sent,
        raw_recv,
        sum_recv,
        relay_send,
        relay_recv,
        local_sem,
        ready,
    ) = names

    d = lax.axis_index("energy")
    y = lax.axis_index("atom")
    core = lax.rem(d, 2)
    has_low, has_high = d >= 2, d < energy_devices - 2
    has_under, has_over = y >= 1, y < atom_devices - 1
    exists = {
        TO_LOW: has_low,
        TO_HIGH: has_high,
        OWN: d >= 0,
        TO_UNDER: has_under,
        TO_OVER: has_over,
    }
    partner = d + 1 - 2 * core
    targets = {
        TO_LOW: (d - 2, y),
        TO_HIGH: (d + 2, y),
        OWN: (partner, y),
        PASSED: (partner, y),
        TO_UNDER: (d, y - 1),
        TO_OVER: (d, y + 1),
    }
    place = lax.rem(d, ROW)
    never = d < 0
    first = (d == 0) & (y == 0)
    leads = {
        TO_LOW: never,
        TO_HIGH: first | (place >= ROW - 2),
        OWN: first,
        TO_UNDER: never,
        TO_OVER: first,
    }
    late = {
        TO_LOW: ((d == 2) & (y == 0)) | ((place < 2) & (d >= ROW)),
        TO_HIGH: never,
        OWN: (d == 1) & (y == 0),
        TO_UNDER: (d == 0) & (y == 1),
        TO_OVER: never,
    }
    meets_z = late[TO_LOW] | late[OWN]
    slow_high = (place >= ROW - 2) & has_high
    late_z = meets_z | slow_high
    early_core = jnp.where(slow_high, 1, 0)
    row = lax.div(d, ROW)
    relays = (place >= ROW - 2) & (d >= ROW)
    greets = (place < 2) & (d >= ROW)
    detours_raw = {chunks - 1: 0, chunks - 2: 1}
    detours_sum = {0: 0, 1: 2}

    def detour(r):
        return slow_high & (row >= detours_raw[r]) if r in detours_raw else never

    def relayed(r):
        return relays & (row >= detours_raw[r] + 1)

    def detour_sum(r):
        return slow_high & (row >= detours_sum[r]) if r in detours_sum else never

    def relayed_sum(r):
        return relays & (row >= detours_sum[r] + 1)

    late_y = late[TO_UNDER]
    pass_out = jnp.where(core == 0, d < energy_devices - 2, d >= 2)
    pass_in = jnp.where(core == 0, d >= 2, d < energy_devices - 2)
    slot_of = {TO_LOW: 6, TO_HIGH: 0, OWN: 2 + 2 * core, PASSED: 4 - 2 * core}
    passed_from = 6 - 6 * core
    kept_from = 6 * core

    barrier = pltpu.get_barrier_semaphore()
    count = jnp.int32(0)
    for kind in (TO_LOW, TO_HIGH, OWN, TO_UNDER, TO_OVER):
        count = count + jnp.where(exists[kind], 1, 0) - jnp.where(late[kind], 1, 0)

        @pl.when(exists[kind] & jnp.logical_not(leads[kind]))
        def _(kind=kind):
            pl.semaphore_signal(barrier, inc=1, device_id=targets[kind], device_id_type=MESH)

    def remote(source, target, send, recv, kind):
        return pltpu.make_async_remote_copy(
            src_ref=source,
            dst_ref=target,
            send_sem=send,
            recv_sem=recv,
            device_id=targets[kind] if isinstance(kind, int) else kind,
            device_id_type=MESH,
        )

    def raw_copy(kind, r):
        send, recv = sent.at[kind], raw_recv.at[ARRIVAL[kind], r]
        if kind in (TO_UNDER, TO_OVER):
            source = green.at[:, :, 1, pl.ds(r * rows, rows), :]
            side = 1 if kind == TO_UNDER else 0
            return remote(source, raw_y[r].at[side], send, recv, kind)
        target = raw_z[r].at[pl.ds(slot_of[kind], 2)]
        if kind == PASSED:
            source = raw_z[r].at[pl.ds(passed_from, 2)]
        else:
            source = green.at[:, :, 0, pl.ds(r * rows, rows), :]
        return remote(source, target, send, recv, kind)

    def sum_copy(kind, a, r):
        index = a * chunks + r
        send, recv = sent.at[kind], sum_recv.at[ARRIVAL[kind], index]
        if kind in (TO_UNDER, TO_OVER):
            side = 1 if kind == TO_UNDER else 0
            return remote(
                sent_y[a][r].at[1 - side], summed_y[a][r].at[side], send, recv, kind
            )
        target = summed_z[a][r].at[pl.ds(slot_of[kind], 2)]
        if kind == PASSED:
            source = summed_z[a][r].at[pl.ds(passed_from, 2)]
        else:
            source = own_sum[a][r]
        return remote(source, target, send, recv, kind)

    def raw_detour(r):
        source = green.at[:, :, 0, pl.ds(r * rows, rows), :]
        send = sent.at[TO_HIGH]
        return remote(source, relay_raw[r], send, relay_recv.at[chunks - 1 - r], (d + ROW, y))

    def sum_detour(a, r):
        index = a * chunks + r
        send, recv = sent.at[TO_HIGH], relay_recv.at[2 + 2 * a + r]
        return remote(own_sum[a][r], relay_sum[a][r], send, recv, (d + ROW, y))

    def raw_relay(r):
        target, recv = raw_z[r].at[0:2], raw_recv.at[TO_HIGH, r]
        return remote(relay_raw[r], target, relay_send.at[chunks - 1 - r], recv, (d - ROW + 2, y))

    def sum_relay(a, r):
        index = a * chunks + r
        send, recv = relay_send.at[2 + 2 * a + r], sum_recv.at[TO_HIGH, index]
        return remote(relay_sum[a][r], summed_z[a][r].at[0:2], send, recv, (d - ROW + 2, y))

    def relay_raw_step(r, condition):
        @pl.when(condition)
        def _():
            raw_detour(r).wait_recv()
            raw_relay(r).start()

    def relay_step(at):
        if at == 0:
            relay_raw_step(chunks - 2, relays & (row >= 2))
            relay_raw_step(chunks - 1, relays & (row == 1))
        if at == 1:
            relay_raw_step(chunks - 1, relays & (row >= 2))
        if at - 2 in detours_sum:
            r = at - 2

            @pl.when(relayed_sum(r))
            def _():
                for a in range(2):
                    sum_detour(a, r).wait_recv()
                    sum_relay(a, r).start()

    def together(place, recv):
        remote(place, place, sent.at[OWN], recv, OWN).wait_recv()

    both_y = has_under & has_over
    single_y = (has_under | has_over) & jnp.logical_not(both_y)

    def raw_arrival(r, start, which):
        place = raw_z[r].at[pl.ds(start, 2)]
        return remote(place, place, sent.at[which], raw_recv.at[which, r], OWN)

    def sum_arrival(a, r, start, which):
        place, index = summed_z[a][r].at[pl.ds(start, 2)], a * chunks + r
        return remote(place, place, sent.at[which], sum_recv.at[which, index], OWN)

    locals_ = [
        pltpu.make_async_copy(source, target, local_sem.at[i])
        for i, (source, target) in enumerate(
            (
                (green_hbm, green),
                (coupling_hbm, coupling),
                (up_hbm, up),
                (down_hbm, down),
                (up_weight_hbm, up_weight),
                (down_weight_hbm, down_weight),
                (neighbours_hbm, neighbours),
                (strength_hbm, strength),
            )
        )
    ]
    for copy in locals_:
        copy.start()

    @pl.when(greets)
    def _():
        pl.semaphore_signal(barrier, inc=1, device_id=(d + ROW - 2, y), device_id_type=MESH)

    @pl.when(relays)
    def _():
        pl.semaphore_signal(barrier, inc=1, device_id=(d - ROW, y), device_id_type=MESH)

    count = count + jnp.where(relays, 1, 0) + jnp.where(slow_high, 1, 0)
    with scope("S_barrier"):
        pl.semaphore_wait(barrier, count)

    for kind in (TO_HIGH, OWN, TO_OVER):

        @pl.when(exists[kind] & leads[kind])
        def _(kind=kind):
            pl.semaphore_signal(ready, inc=1, device_id=targets[kind], device_id_type=MESH)

    locals_[0].wait()
    for kind in (TO_LOW, TO_HIGH, TO_UNDER, TO_OVER, OWN):

        @pl.when(exists[kind] & jnp.logical_not(late[kind]))
        def _(kind=kind):
            for r in range(chunks):
                if kind != TO_HIGH or r not in detours_raw:
                    raw_copy(kind, r).start()
                    continue

                @pl.when(detour(r))
                def _(r=r):
                    raw_detour(r).start()

                @pl.when(jnp.logical_not(detour(r)))
                def _(r=r):
                    raw_copy(TO_HIGH, r).start()

    def clear(condition, refs):
        @pl.when(jnp.logical_not(condition))
        def _():
            for ref in refs:
                ref[...] = jnp.zeros(ref.shape, ref.dtype)

    flat_z = [ref for a in range(2) for ref in summed_z[a]]
    flat_y = [ref for a in range(2) for ref in summed_y[a]]
    clear(has_low, [ref.at[0:2] for ref in raw_z + flat_z])
    clear(has_high, [ref.at[6:8] for ref in raw_z + flat_z])
    clear(has_under, [ref.at[0] for ref in raw_y + flat_y])
    clear(has_over, [ref.at[1] for ref in raw_y + flat_y])

    with scope("S_localwait"):
        for copy in locals_[1:]:
            copy.wait()

    clusters = 2 * atom_devices
    first_energy = 2 * d
    first_cluster = 2 * y

    def table(a, b):
        row = lax.rem(a + clusters, clusters)
        inside = (a >= 0) & (a < clusters) & (b >= 0) & (b < clusters)
        total = jnp.float32(0.0)
        for j in range(neighbours.shape[0]):
            total = total + jnp.where(neighbours[j, row] == b, strength[j, row], jnp.float32(0.0))
        return jnp.where(inside, total, jnp.float32(0.0))

    def entry(a, b):
        return table(first_cluster + a, first_cluster + b)

    reach = {
        (a, b): entry(a, b) for a in range(-2, 4) for b in range(-2, 4)
        if abs(a - b) <= 2 and (0 <= a < 2 or 0 <= b < 2)
    }

    up_slot, down_slot, up_factor, down_factor = [], [], [], []
    for e in range(2):
        u, l = up[e], down[e]
        up_slot.append(jnp.where(u >= 0, jnp.minimum(jnp.maximum(u - first_energy + 2, 4), 7), 7))
        down_slot.append(jnp.where(l >= 0, jnp.minimum(jnp.maximum(l - first_energy + 4, 0), 3), 0))
        up_factor.append(jnp.where(u >= 0, up_weight[e], jnp.float32(0.0)))
        down_factor.append(jnp.where(l >= 0, down_weight[e], jnp.float32(0.0)))

    def dot(left, right):
        return jnp.dot(left, right, preferred_element_type=F32)

    scale = 1.0 / (2.0 * orbitals)
    for a in range(2):
        turned = coupling[a].T
        for e in range(2):
            for part in range(2):
                x = dot(turned, green[e, a, part]) * scale
                x_big[a, e, 0:orbitals, part * orbitals : (part + 1) * orbitals] = x.astype(BF16)
                other = -x if part == 1 else x
                x_big[a, e, orbitals:, (1 - part) * orbitals : (2 - part) * orbitals] = other.astype(BF16)
                gc[a, e, :, part * orbitals : (part + 1) * orbitals] = dot(
                    green[e, a, part], coupling[a]
                ).astype(BF16)

    def wide(value):
        return value.astype(F32)

    def cluster_sums(r):
        span = pl.ds(r * rows, rows)
        for e in range(2):
            terms = {
                -2: wide(raw_y[r][0, e, 0]),
                -1: wide(raw_y[r][0, e, 1]),
                0: wide(green[e, 0, 1, span, :]),
                1: wide(green[e, 1, 1, span, :]),
                2: wide(raw_y[r][1, e, 0]),
                3: wide(raw_y[r][1, e, 1]),
            }
            for a in range(2):
                total = None
                for b in range(a - 2, a + 3):
                    piece = reach[a, b] * terms[b]
                    total = piece if total is None else total + piece
                own_sum[a][r][e] = total.astype(BF16)

    def energy_sums(r):
        for e in range(2):
            values = []
            for c in range(2):
                value = (
                    up_factor[e] * wide(raw_z[r][up_slot[e], c])
                    + down_factor[e] * wide(raw_z[r][down_slot[e], c])
                ).astype(BF16)
                hidden[r][e, c] = value
                values.append(wide(value))
            sent_y[0][r][0, e] = (reach[-2, 0] * values[0]).astype(BF16)
            sent_y[1][r][0, e] = (reach[-1, 0] * values[0] + reach[-1, 1] * values[1]).astype(BF16)
            sent_y[0][r][1, e] = (reach[2, 0] * values[0] + reach[2, 1] * values[1]).astype(BF16)
            sent_y[1][r][1, e] = (reach[3, 1] * values[1]).astype(BF16)

    def start_sums(kinds, a, r, only=None, extra=None):
        for kind in kinds:
            condition = exists[kind] if extra is None else exists[kind] & extra
            if only is not None:
                condition = late[kind] if only else condition & jnp.logical_not(late[kind])
            if kind == TO_HIGH and r in detours_sum and only is not True:
                condition = condition & jnp.logical_not(detour_sum(r))

            @pl.when(condition)
            def _(kind=kind):
                sum_copy(kind, a, r).start()

    def pass_raw(r, whose=None):
        @pl.when(pass_out if whose is None else pass_out & (core == whose))
        def _():
            with scope(f"W_zraw{r}"):
                raw_arrival(r, passed_from, core).wait_recv()
            raw_copy(PASSED, r).start()

    def over_energies(r, only=None):
        @pl.when(jnp.logical_not(pass_in))
        def _():
            raw_copy(OWN, r).wait_recv()

        @pl.when(pass_in)
        def _():
            with scope(f"W_pass{r}"):
                raw_arrival(r, kept_from, 1 - core).wait_recv()
                together(raw_z[r].at[2:6], raw_recv.at[2, r])

        energy_sums(r)
        start_sums(OVER_Y, 0, r, only)

    def over_clusters(r, only=None):
        with scope(f"W_yraw{r}"):

            @pl.when(both_y)
            def _():
                together(raw_y[r], raw_recv.at[3, r])

            @pl.when(single_y)
            def _():
                raw_copy(TO_OVER, r).wait_recv()

        cluster_sums(r)
        start_sums(OVER_Z, 0, r, only)

    def meet(kinds):
        pl.semaphore_wait(ready, 1)
        for kind in kinds:

            @pl.when(late[kind])
            def _(kind=kind):
                for r in range(chunks):
                    raw_copy(kind, r).start()

    @pl.when(jnp.logical_not(late_y | late_z))
    def _():
        for r in range(chunks):
            pass_raw(r)
            if r:
                over_energies(r - 1)
            over_clusters(r)
            relay_step(r)
        for r in range(chunks):
            start_sums(OVER_Z, 1, r)
        start_sums(OVER_Y, 1, 0)
        over_energies(chunks - 1)
        for r in range(1, chunks):
            start_sums(OVER_Y, 1, r)

    @pl.when(late_y)
    def _():
        for r in range(chunks):
            pass_raw(r)
            if r:
                over_energies(r - 1, False)
                if r == 1:
                    meet(OVER_Y)
                start_sums(OVER_Y, 0, r - 1, True)
        start_sums(OVER_Y, 1, 0)
        over_energies(chunks - 1)
        for r in range(1, chunks):
            start_sums(OVER_Y, 1, r)
        for r in range(chunks):
            over_clusters(r)
        for r in range(chunks):
            start_sums(OVER_Z, 1, r)

    @pl.when(late_z)
    def _():
        for r in range(chunks):
            pass_raw(r, early_core)
            over_clusters(r, False)
            if r == 0:

                @pl.when(meets_z)
                def _():
                    meet(OVER_Z)

            if r in detours_sum:

                @pl.when(detour_sum(r))
                def _(r=r):
                    for a in range(2):
                        sum_detour(a, r).start()

            start_sums(OVER_Z, 0, r, True)
            start_sums(OVER_Z, 1, r)
            relay_step(r)
        for r in range(chunks):
            pass_raw(r, 1 - early_core)
            if r:
                over_energies(r - 1)
                start_sums(OVER_Y, 1, r - 1, extra=greets)
        others = jnp.logical_not(greets)
        start_sums(OVER_Y, 1, 0, extra=others)
        over_energies(chunks - 1)
        for r in range(1, chunks - 1):
            start_sums(OVER_Y, 1, r, extra=others)
        start_sums(OVER_Y, 1, chunks - 1)

    def read(a, r):
        span = pl.ds(r * rows, rows)
        with scope(f"W_ysum{a}{r}"):

            @pl.when(both_y)
            def _():
                together(summed_y[a][r], sum_recv.at[3, a * chunks + r])

            @pl.when(single_y)
            def _():
                sum_copy(TO_OVER, a, r).wait_recv()

        for e in range(2):
            total = wide(summed_y[a][r][0, e]) + wide(summed_y[a][r][1, e])
            for c in range(2):
                total = total + reach[a, c] * wide(hidden[r][e, c])
            reader[a, e, :, 0:orbitals] = total.astype(BF16)
        with scope(f"W_zpass{a}{r}"):

            @pl.when(jnp.logical_not(pass_in))
            def _():
                sum_copy(OWN, a, r).wait_recv()

            @pl.when(pass_in)
            def _():
                sum_arrival(a, r, kept_from, 1 - core).wait_recv()
                together(summed_z[a][r].at[2:6], sum_recv.at[2, a * chunks + r])

        for e in range(2):
            total = up_factor[e] * wide(summed_z[a][r][up_slot[e]]) + down_factor[e] * wide(
                summed_z[a][r][down_slot[e]]
            )
            reader[a, e, :, orbitals:] = total.astype(BF16)
        for e in range(2):
            value = dot(reader[a, e], x_big[a, e])
            real, imag = value[:, :orbitals].astype(BF16), value[:, orbitals:].astype(BF16)
            after = pl.ds(orbitals + r * rows, rows)
            y_big[a, e, span, 0:orbitals] = real
            y_big[a, e, span, orbitals:] = imag
            y_big[a, e, after, 0:orbitals] = -imag
            y_big[a, e, after, orbitals:] = real

    def finish(a):
        for e in range(2):
            first = dot(coupling[a], y_big[a, e, 0:orbitals])
            real, imag = first[:, :orbitals].astype(BF16), first[:, orbitals:].astype(BF16)
            f_big[e, 0:orbitals, 0:orbitals] = real
            f_big[e, 0:orbitals, orbitals:] = imag
            f_big[e, orbitals:, 0:orbitals] = -imag
            f_big[e, orbitals:, orbitals:] = real
        for e in range(2):
            second_cat[e] = dot(gc[a, e], y_big[a, e])
        for e in range(2):
            third = dot(second_cat[e].astype(BF16), f_big[e])
            for part in range(2):
                side = slice(part * orbitals, (part + 1) * orbitals)
                out_ref[e, a, part] = (
                    wide(green[e, a, part]) + second_cat[e, :, side] + third[:, side]
                ).astype(BF16)

    def pass_sum(a, r, condition):
        @pl.when(condition)
        def _():
            with scope(f"W_zsum{a}{r}"):
                sum_arrival(a, r, passed_from, core).wait_recv()
            sum_copy(PASSED, a, r).start()

    @pl.when(jnp.logical_not(greets))
    def _():
        steps = [(a, r) for a in range(2) for r in range(chunks)]
        for at, (a, r) in enumerate(steps):
            pass_sum(a, r, pass_out)
            if at:
                read(*steps[at - 1])
                if steps[at - 1][1] == chunks - 1:
                    finish(steps[at - 1][0])
        read(*steps[-1])
        finish(1)

    @pl.when(greets)
    def _():
        last = chunks - 1
        lower, upper = pass_out & (core == 0), pass_out & (core == 1)

        @pl.when(lower)
        def _():
            for a in range(2):
                for r in range(chunks):
                    sum_arrival(a, r, passed_from, core).wait_recv()
                    sum_copy(PASSED, a, r).start()

        for r in range(1, last):
            for a in range(2):
                pass_sum(a, r, upper)
            for a in range(2):
                read(a, r)
        for a in range(2):
            pass_sum(a, 0, upper)
        read(0, 0)
        pass_sum(0, last, upper)
        read(1, 0)
        pass_sum(1, last, upper)
        read(0, last)
        finish(0)
        read(1, last)
        finish(1)

    with scope("S_sends"):
        for kind in range(6):

            @pl.when(pass_out if kind == PASSED else exists[kind])
            def _(kind=kind):
                remote(green, green, sent.at[kind], raw_recv.at[0, 0], OWN).wait_send()

        for r in detours_raw:

            @pl.when(relayed(r))
            def _(r=r):
                raw_relay(r).wait_send()

        for r in detours_sum:

            @pl.when(relayed_sum(r))
            def _(r=r):
                for a in range(2):
                    sum_relay(a, r).wait_send()


def solution(mesh):
    energy_devices, atom_devices = mesh.shape["energy"], mesh.shape["atom"]

    def on_device(
        green_blocks, coupling, up_partner, down_partner, up_weight, down_weight, neighbours, strength
    ):
        orbitals = green_blocks.shape[-1]
        rows = orbitals // CHUNKS
        slots = neighbours.shape[1]
        clusters = neighbours.shape[0]

        def vmem(*shape, dtype=BF16):
            return pltpu.VMEM(shape, dtype)

        many = range(CHUNKS)
        scratch = (
            [vmem(8, 2, rows, orbitals) for _ in many]
            + [vmem(2, 2, 2, rows, orbitals) for _ in many]
            + [vmem(8, rows, orbitals) for _ in range(2 * CHUNKS)]
            + [vmem(2, 2, rows, orbitals) for _ in range(2 * CHUNKS)]
            + [vmem(2, rows, orbitals) for _ in range(2 * CHUNKS)]
            + [vmem(2, 2, rows, orbitals) for _ in many]
            + [vmem(2, 2, rows, orbitals) for _ in range(2)]
            + [vmem(2, rows, orbitals) for _ in range(4)]
            + [vmem(2, 2, rows, orbitals) for _ in range(2 * CHUNKS)]
            + [
                vmem(2, 2, 2, orbitals, orbitals),
                vmem(2, orbitals, orbitals),
                pltpu.SMEM((2,), jnp.int32),
                pltpu.SMEM((2,), jnp.int32),
                pltpu.SMEM((2,), F32),
                pltpu.SMEM((2,), F32),
                pltpu.SMEM((slots, clusters), jnp.int32),
                pltpu.SMEM((slots, clusters), F32),
                vmem(2, 2, rows, 2 * orbitals),
                vmem(2, 2, 2 * orbitals, 2 * orbitals),
                vmem(2, 2, orbitals, 2 * orbitals),
                vmem(2, 2, 2 * orbitals, 2 * orbitals),
                vmem(2, 2 * orbitals, 2 * orbitals),
                vmem(2, orbitals, 2 * orbitals, dtype=F32),
                pltpu.SemaphoreType.DMA((6,)),
                pltpu.SemaphoreType.DMA((4, CHUNKS)),
                pltpu.SemaphoreType.DMA((4, 2 * CHUNKS)),
                pltpu.SemaphoreType.DMA((6,)),
                pltpu.SemaphoreType.DMA((6,)),
                pltpu.SemaphoreType.DMA((8,)),
                pltpu.SemaphoreType.REGULAR,
            ]
        )
        return pl.pallas_call(
            functools.partial(kernel, energy_devices, atom_devices),
            out_shape=jax.ShapeDtypeStruct(green_blocks.shape, green_blocks.dtype),
            in_specs=[pl.BlockSpec(memory_space=pl.ANY)] * 8,
            out_specs=pl.BlockSpec(memory_space=pltpu.VMEM),
            scratch_shapes=scratch,
            compiler_params=pltpu.CompilerParams(
                collective_id=0, has_side_effects=True, vmem_limit_bytes=24 * 1024 * 1024
            ),
            name="update",
        )(
            *(
                pltpu.with_memory_space_constraint(array, pltpu.HBM)
                for array in (
                    green_blocks,
                    coupling,
                    up_partner,
                    down_partner,
                    up_weight,
                    down_weight,
                    neighbours.T,
                    strength.T,
                )
            )
        )

    in_specs = (
        P("energy", "atom", None, None, None),
        P("atom", None, None),
        P("energy"),
        P("energy"),
        P("energy"),
        P("energy"),
        P(),
        P(),
    )
    out_specs = P("energy", "atom", None, None, None)
    return jax.shard_map(
        on_device, mesh=mesh, in_specs=in_specs, out_specs=out_specs, check_vma=False
    )
```

```python
import functools

import jax
import jax.numpy as jnp
from jax import lax
from jax.experimental import pallas as pl
from jax.experimental.pallas import tpu as pltpu
from jax.sharding import PartitionSpec as P

MESH = pl.DeviceIdType.MESH
CHUNKS = 4
ROW = 24
F32 = jnp.float32
BF16 = jnp.bfloat16

TO_LOW, TO_HIGH, OWN, PASSED, TO_UNDER, TO_OVER = range(6)
ARRIVAL = (0, 1, 2, 2, 3, 3)
OVER_Z = (TO_LOW, TO_HIGH, OWN)
OVER_Y = (TO_UNDER, TO_OVER)
scope = jax.named_scope


def kernel(
    energy_devices,
    atom_devices,
    green_hbm,
    coupling_hbm,
    up_hbm,
    down_hbm,
    up_weight_hbm,
    down_weight_hbm,
    neighbours_hbm,
    strength_hbm,
    out_ref,
    *scratch,
):
    chunks = CHUNKS
    orbitals = green_hbm.shape[-1]
    rows = orbitals // chunks
    names = iter(scratch)

    def take(count):
        return [next(names) for _ in range(count)]

    raw_z = take(chunks)
    raw_y = take(chunks)
    summed_z = [take(chunks) for _ in range(2)]
    summed_y = [take(chunks) for _ in range(2)]
    own_sum = [take(chunks) for _ in range(2)]
    hidden = take(chunks)
    relay_raw = dict(zip((chunks - 2, chunks - 1), take(2)))
    relay_sum = [take(2) for _ in range(2)]
    sent_y = [take(chunks) for _ in range(2)]
    (
        green,
        coupling,
        up,
        down,
        up_weight,
        down_weight,
        neighbours,
        strength,
        reader,
        x_big,
        gc,
        y_big,
        f_big,
        second_cat,
        sent,
        raw_recv,
        sum_recv,
        relay_send,
        relay_recv,
        local_sem,
        ready,
    ) = names

    d = lax.axis_index("energy")
    y = lax.axis_index("atom")
    core = lax.rem(d, 2)
    has_low, has_high = d >= 2, d < energy_devices - 2
    has_under, has_over = y >= 1, y < atom_devices - 1
    exists = {
        TO_LOW: has_low,
        TO_HIGH: has_high,
        OWN: d >= 0,
        TO_UNDER: has_under,
        TO_OVER: has_over,
    }
    partner = d + 1 - 2 * core
    targets = {
        TO_LOW: (d - 2, y),
        TO_HIGH: (d + 2, y),
        OWN: (partner, y),
        PASSED: (partner, y),
        TO_UNDER: (d, y - 1),
        TO_OVER: (d, y + 1),
    }
    place = lax.rem(d, ROW)
    never = d < 0
    first = (d == 0) & (y == 0)
    leads = {
        TO_LOW: never,
        TO_HIGH: first | (place >= ROW - 2),
        OWN: first,
        TO_UNDER: never,
        TO_OVER: first,
    }
    late = {
        TO_LOW: ((d == 2) & (y == 0)) | ((place < 2) & (d >= ROW)),
        TO_HIGH: never,
        OWN: (d == 1) & (y == 0),
        TO_UNDER: (d == 0) & (y == 1),
        TO_OVER: never,
    }
    meets_z = late[TO_LOW] | late[OWN]
    slow_high = (place >= ROW - 2) & has_high
    late_z = meets_z | slow_high
    early_core = jnp.where(slow_high, 1, 0)
    row = lax.div(d, ROW)
    relays = (place >= ROW - 2) & (d >= ROW)
    greets = (place < 2) & (d >= ROW)
    detours_raw = {chunks - 1: 0, chunks - 2: 1}
    detours_sum = {0: 0, 1: 2}

    def detour(r):
        return slow_high & (row >= detours_raw[r]) if r in detours_raw else never

    def relayed(r):
        return relays & (row >= detours_raw[r] + 1)

    def detour_sum(r):
        return slow_high & (row >= detours_sum[r]) if r in detours_sum else never

    def relayed_sum(r):
        return relays & (row >= detours_sum[r] + 1)

    late_y = late[TO_UNDER]
    pass_out = jnp.where(core == 0, d < energy_devices - 2, d >= 2)
    pass_in = jnp.where(core == 0, d >= 2, d < energy_devices - 2)
    slot_of = {TO_LOW: 6, TO_HIGH: 0, OWN: 2 + 2 * core, PASSED: 4 - 2 * core}
    passed_from = 6 - 6 * core
    kept_from = 6 * core

    barrier = pltpu.get_barrier_semaphore()
    count = jnp.int32(0)
    for kind in (TO_LOW, TO_HIGH, OWN, TO_UNDER, TO_OVER):
        count = count + jnp.where(exists[kind], 1, 0) - jnp.where(late[kind], 1, 0)

        @pl.when(exists[kind] & jnp.logical_not(leads[kind]))
        def _(kind=kind):
            pl.semaphore_signal(barrier, inc=1, device_id=targets[kind], device_id_type=MESH)

    def remote(source, target, send, recv, kind):
        return pltpu.make_async_remote_copy(
            src_ref=source,
            dst_ref=target,
            send_sem=send,
            recv_sem=recv,
            device_id=targets[kind] if isinstance(kind, int) else kind,
            device_id_type=MESH,
        )

    def raw_copy(kind, r):
        send, recv = sent.at[kind], raw_recv.at[ARRIVAL[kind], r]
        if kind in (TO_UNDER, TO_OVER):
            source = green.at[:, :, 1, pl.ds(r * rows, rows), :]
            side = 1 if kind == TO_UNDER else 0
            return remote(source, raw_y[r].at[side], send, recv, kind)
        target = raw_z[r].at[pl.ds(slot_of[kind], 2)]
        if kind == PASSED:
            source = raw_z[r].at[pl.ds(passed_from, 2)]
        else:
            source = green.at[:, :, 0, pl.ds(r * rows, rows), :]
        return remote(source, target, send, recv, kind)

    def sum_copy(kind, a, r):
        index = a * chunks + r
        send, recv = sent.at[kind], sum_recv.at[ARRIVAL[kind], index]
        if kind in (TO_UNDER, TO_OVER):
            side = 1 if kind == TO_UNDER else 0
            return remote(
                sent_y[a][r].at[1 - side], summed_y[a][r].at[side], send, recv, kind
            )
        target = summed_z[a][r].at[pl.ds(slot_of[kind], 2)]
        if kind == PASSED:
            source = summed_z[a][r].at[pl.ds(passed_from, 2)]
        else:
            source = own_sum[a][r]
        return remote(source, target, send, recv, kind)

    def raw_detour(r):
        source = green.at[:, :, 0, pl.ds(r * rows, rows), :]
        send = sent.at[TO_HIGH]
        return remote(source, relay_raw[r], send, relay_recv.at[chunks - 1 - r], (d + ROW, y))

    def sum_detour(a, r):
        index = a * chunks + r
        send, recv = sent.at[TO_HIGH], relay_recv.at[2 + 2 * a + r]
        return remote(own_sum[a][r], relay_sum[a][r], send, recv, (d + ROW, y))

    def raw_relay(r):
        target, recv = raw_z[r].at[0:2], raw_recv.at[TO_HIGH, r]
        return remote(relay_raw[r], target, relay_send.at[chunks - 1 - r], recv, (d - ROW + 2, y))

    def sum_relay(a, r):
        index = a * chunks + r
        send, recv = relay_send.at[2 + 2 * a + r], sum_recv.at[TO_HIGH, index]
        return remote(relay_sum[a][r], summed_z[a][r].at[0:2], send, recv, (d - ROW + 2, y))

    def relay_raw_step(r, condition):
        @pl.when(condition)
        def _():
            raw_detour(r).wait_recv()
            raw_relay(r).start()

    def relay_step(at):
        if at == 0:
            relay_raw_step(chunks - 2, relays & (row >= 2))
            relay_raw_step(chunks - 1, relays & (row == 1))
        if at == 1:
            relay_raw_step(chunks - 1, relays & (row >= 2))
        if at - 2 in detours_sum:
            r = at - 2

            @pl.when(relayed_sum(r))
            def _():
                for a in range(2):
                    sum_detour(a, r).wait_recv()
                    sum_relay(a, r).start()

    def together(place, recv):
        remote(place, place, sent.at[OWN], recv, OWN).wait_recv()

    both_y = has_under & has_over
    single_y = (has_under | has_over) & jnp.logical_not(both_y)

    def raw_arrival(r, start, which):
        place = raw_z[r].at[pl.ds(start, 2)]
        return remote(place, place, sent.at[which], raw_recv.at[which, r], OWN)

    def sum_arrival(a, r, start, which):
        place, index = summed_z[a][r].at[pl.ds(start, 2)], a * chunks + r
        return remote(place, place, sent.at[which], sum_recv.at[which, index], OWN)

    locals_ = [
        pltpu.make_async_copy(source, target, local_sem.at[i])
        for i, (source, target) in enumerate(
            (
                (green_hbm, green),
                (coupling_hbm, coupling),
                (up_hbm, up),
                (down_hbm, down),
                (up_weight_hbm, up_weight),
                (down_weight_hbm, down_weight),
                (neighbours_hbm, neighbours),
                (strength_hbm, strength),
            )
        )
    ]
    for copy in locals_:
        copy.start()

    @pl.when(greets)
    def _():
        pl.semaphore_signal(barrier, inc=1, device_id=(d + ROW - 2, y), device_id_type=MESH)

    @pl.when(relays)
    def _():
        pl.semaphore_signal(barrier, inc=1, device_id=(d - ROW, y), device_id_type=MESH)

    count = count + jnp.where(relays, 1, 0) + jnp.where(slow_high, 1, 0)
    with scope("S_barrier"):
        pl.semaphore_wait(barrier, count)

    for kind in (TO_HIGH, OWN, TO_OVER):

        @pl.when(exists[kind] & leads[kind])
        def _(kind=kind):
            pl.semaphore_signal(ready, inc=1, device_id=targets[kind], device_id_type=MESH)

    locals_[0].wait()
    for kind in (TO_UNDER, TO_OVER, TO_HIGH, TO_LOW, OWN):

        @pl.when(exists[kind] & jnp.logical_not(late[kind]))
        def _(kind=kind):
            for r in range(chunks):
                if kind != TO_HIGH or r not in detours_raw:
                    raw_copy(kind, r).start()
                    continue

                @pl.when(detour(r))
                def _(r=r):
                    raw_detour(r).start()

                @pl.when(jnp.logical_not(detour(r)))
                def _(r=r):
                    raw_copy(TO_HIGH, r).start()

    def clear(condition, refs):
        @pl.when(jnp.logical_not(condition))
        def _():
            for ref in refs:
                ref[...] = jnp.zeros(ref.shape, ref.dtype)

    flat_z = [ref for a in range(2) for ref in summed_z[a]]
    flat_y = [ref for a in range(2) for ref in summed_y[a]]
    clear(has_low, [ref.at[0:2] for ref in raw_z + flat_z])
    clear(has_high, [ref.at[6:8] for ref in raw_z + flat_z])
    clear(has_under, [ref.at[0] for ref in raw_y + flat_y])
    clear(has_over, [ref.at[1] for ref in raw_y + flat_y])

    with scope("S_localwait"):
        for copy in locals_[1:]:
            copy.wait()

    clusters = 2 * atom_devices
    first_energy = 2 * d
    first_cluster = 2 * y

    def table(a, b):
        row = lax.rem(a + clusters, clusters)
        inside = (a >= 0) & (a < clusters) & (b >= 0) & (b < clusters)
        total = jnp.float32(0.0)
        for j in range(neighbours.shape[0]):
            total = total + jnp.where(neighbours[j, row] == b, strength[j, row], jnp.float32(0.0))
        return jnp.where(inside, total, jnp.float32(0.0))

    def entry(a, b):
        return table(first_cluster + a, first_cluster + b)

    reach = {
        (a, b): entry(a, b) for a in range(-2, 4) for b in range(-2, 4)
        if abs(a - b) <= 2 and (0 <= a < 2 or 0 <= b < 2)
    }

    up_slot, down_slot, up_factor, down_factor = [], [], [], []
    for e in range(2):
        u, l = up[e], down[e]
        up_slot.append(jnp.where(u >= 0, jnp.minimum(jnp.maximum(u - first_energy + 2, 4), 7), 7))
        down_slot.append(jnp.where(l >= 0, jnp.minimum(jnp.maximum(l - first_energy + 4, 0), 3), 0))
        up_factor.append(jnp.where(u >= 0, up_weight[e], jnp.float32(0.0)))
        down_factor.append(jnp.where(l >= 0, down_weight[e], jnp.float32(0.0)))

    def dot(left, right):
        return jnp.dot(left, right, preferred_element_type=F32)

    scale = 1.0 / (2.0 * orbitals)
    for a in range(2):
        turned = coupling[a].T
        for e in range(2):
            for part in range(2):
                x = dot(turned, green[e, a, part]) * scale
                x_big[a, e, 0:orbitals, part * orbitals : (part + 1) * orbitals] = x.astype(BF16)
                other = -x if part == 1 else x
                x_big[a, e, orbitals:, (1 - part) * orbitals : (2 - part) * orbitals] = other.astype(BF16)
                gc[a, e, :, part * orbitals : (part + 1) * orbitals] = dot(
                    green[e, a, part], coupling[a]
                ).astype(BF16)

    def wide(value):
        return value.astype(F32)

    def cluster_sums(r):
        span = pl.ds(r * rows, rows)
        for e in range(2):
            terms = {
                -2: wide(raw_y[r][0, e, 0]),
                -1: wide(raw_y[r][0, e, 1]),
                0: wide(green[e, 0, 1, span, :]),
                1: wide(green[e, 1, 1, span, :]),
                2: wide(raw_y[r][1, e, 0]),
                3: wide(raw_y[r][1, e, 1]),
            }
            for a in range(2):
                total = None
                for b in range(a - 2, a + 3):
                    piece = reach[a, b] * terms[b]
                    total = piece if total is None else total + piece
                own_sum[a][r][e] = total.astype(BF16)

    def energy_sums(r):
        for e in range(2):
            values = []
            for c in range(2):
                value = (
                    up_factor[e] * wide(raw_z[r][up_slot[e], c])
                    + down_factor[e] * wide(raw_z[r][down_slot[e], c])
                ).astype(BF16)
                hidden[r][e, c] = value
                values.append(wide(value))
            sent_y[0][r][0, e] = (reach[-2, 0] * values[0]).astype(BF16)
            sent_y[1][r][0, e] = (reach[-1, 0] * values[0] + reach[-1, 1] * values[1]).astype(BF16)
            sent_y[0][r][1, e] = (reach[2, 0] * values[0] + reach[2, 1] * values[1]).astype(BF16)
            sent_y[1][r][1, e] = (reach[3, 1] * values[1]).astype(BF16)

    def start_sums(kinds, a, r, only=None, extra=None):
        for kind in kinds:
            condition = exists[kind] if extra is None else exists[kind] & extra
            if only is not None:
                condition = late[kind] if only else condition & jnp.logical_not(late[kind])
            if kind == TO_HIGH and r in detours_sum and only is not True:
                condition = condition & jnp.logical_not(detour_sum(r))

            @pl.when(condition)
            def _(kind=kind):
                sum_copy(kind, a, r).start()

    def pass_raw(r, whose=None):
        @pl.when(pass_out if whose is None else pass_out & (core == whose))
        def _():
            with scope(f"W_zraw{r}"):
                raw_arrival(r, passed_from, core).wait_recv()
            raw_copy(PASSED, r).start()

    def over_energies(r, only=None):
        @pl.when(jnp.logical_not(pass_in))
        def _():
            raw_copy(OWN, r).wait_recv()

        @pl.when(pass_in)
        def _():
            with scope(f"W_pass{r}"):
                raw_arrival(r, kept_from, 1 - core).wait_recv()
                together(raw_z[r].at[2:6], raw_recv.at[2, r])

        energy_sums(r)
        start_sums(OVER_Y, 0, r, only)

    def over_clusters(r, only=None):
        with scope(f"W_yraw{r}"):

            @pl.when(both_y)
            def _():
                together(raw_y[r], raw_recv.at[3, r])

            @pl.when(single_y)
            def _():
                raw_copy(TO_OVER, r).wait_recv()

        cluster_sums(r)
        start_sums(OVER_Z, 0, r, only)

    def meet(kinds):
        pl.semaphore_wait(ready, 1)
        for kind in kinds:

            @pl.when(late[kind])
            def _(kind=kind):
                for r in range(chunks):
                    raw_copy(kind, r).start()

    @pl.when(jnp.logical_not(late_y | late_z))
    def _():
        for r in range(chunks):
            pass_raw(r)
            if r:
                over_energies(r - 1)
            over_clusters(r)
            relay_step(r)
        for r in range(chunks):
            start_sums(OVER_Z, 1, r)
        start_sums(OVER_Y, 1, 0)
        over_energies(chunks - 1)
        for r in range(1, chunks):
            start_sums(OVER_Y, 1, r)

    @pl.when(late_y)
    def _():
        for r in range(chunks):
            pass_raw(r)
            if r:
                over_energies(r - 1, False)
                if r == 1:
                    meet(OVER_Y)
                start_sums(OVER_Y, 0, r - 1, True)
        start_sums(OVER_Y, 1, 0)
        over_energies(chunks - 1)
        for r in range(1, chunks):
            start_sums(OVER_Y, 1, r)
        for r in range(chunks):
            over_clusters(r)
        for r in range(chunks):
            start_sums(OVER_Z, 1, r)

    @pl.when(late_z)
    def _():
        for r in range(chunks):
            pass_raw(r, early_core)
            over_clusters(r, False)
            if r == 0:

                @pl.when(meets_z)
                def _():
                    meet(OVER_Z)

            if r in detours_sum:

                @pl.when(detour_sum(r))
                def _(r=r):
                    for a in range(2):
                        sum_detour(a, r).start()

            start_sums(OVER_Z, 0, r, True)
            start_sums(OVER_Z, 1, r)
            relay_step(r)
        for r in range(chunks):
            pass_raw(r, 1 - early_core)
            if r:
                over_energies(r - 1)
                start_sums(OVER_Y, 1, r - 1, extra=greets)
        others = jnp.logical_not(greets)
        start_sums(OVER_Y, 1, 0, extra=others)
        over_energies(chunks - 1)
        for r in range(1, chunks - 1):
            start_sums(OVER_Y, 1, r, extra=others)
        start_sums(OVER_Y, 1, chunks - 1)

    def read(a, r):
        span = pl.ds(r * rows, rows)
        with scope(f"W_ysum{a}{r}"):

            @pl.when(both_y)
            def _():
                together(summed_y[a][r], sum_recv.at[3, a * chunks + r])

            @pl.when(single_y)
            def _():
                sum_copy(TO_OVER, a, r).wait_recv()

        for e in range(2):
            total = wide(summed_y[a][r][0, e]) + wide(summed_y[a][r][1, e])
            for c in range(2):
                total = total + reach[a, c] * wide(hidden[r][e, c])
            reader[a, e, :, 0:orbitals] = total.astype(BF16)
        with scope(f"W_zpass{a}{r}"):

            @pl.when(jnp.logical_not(pass_in))
            def _():
                sum_copy(OWN, a, r).wait_recv()

            @pl.when(pass_in)
            def _():
                sum_arrival(a, r, kept_from, 1 - core).wait_recv()
                together(summed_z[a][r].at[2:6], sum_recv.at[2, a * chunks + r])

        for e in range(2):
            total = up_factor[e] * wide(summed_z[a][r][up_slot[e]]) + down_factor[e] * wide(
                summed_z[a][r][down_slot[e]]
            )
            reader[a, e, :, orbitals:] = total.astype(BF16)
        for e in range(2):
            value = dot(reader[a, e], x_big[a, e])
            real, imag = value[:, :orbitals].astype(BF16), value[:, orbitals:].astype(BF16)
            after = pl.ds(orbitals + r * rows, rows)
            y_big[a, e, span, 0:orbitals] = real
            y_big[a, e, span, orbitals:] = imag
            y_big[a, e, after, 0:orbitals] = -imag
            y_big[a, e, after, orbitals:] = real

    def finish(a):
        for e in range(2):
            first = dot(coupling[a], y_big[a, e, 0:orbitals])
            real, imag = first[:, :orbitals].astype(BF16), first[:, orbitals:].astype(BF16)
            f_big[e, 0:orbitals, 0:orbitals] = real
            f_big[e, 0:orbitals, orbitals:] = imag
            f_big[e, orbitals:, 0:orbitals] = -imag
            f_big[e, orbitals:, orbitals:] = real
        for e in range(2):
            second_cat[e] = dot(gc[a, e], y_big[a, e])
        for e in range(2):
            third = dot(second_cat[e].astype(BF16), f_big[e])
            for part in range(2):
                side = slice(part * orbitals, (part + 1) * orbitals)
                out_ref[e, a, part] = (
                    wide(green[e, a, part]) + second_cat[e, :, side] + third[:, side]
                ).astype(BF16)

    def pass_sum(a, r, condition):
        @pl.when(condition)
        def _():
            with scope(f"W_zsum{a}{r}"):
                sum_arrival(a, r, passed_from, core).wait_recv()
            sum_copy(PASSED, a, r).start()

    @pl.when(jnp.logical_not(greets))
    def _():
        steps = [(a, r) for a in range(2) for r in range(chunks)]
        for at, (a, r) in enumerate(steps):
            pass_sum(a, r, pass_out)
            if at:
                read(*steps[at - 1])
                if steps[at - 1][1] == chunks - 1:
                    finish(steps[at - 1][0])
        read(*steps[-1])
        finish(1)

    @pl.when(greets)
    def _():
        last = chunks - 1
        lower, upper = pass_out & (core == 0), pass_out & (core == 1)

        @pl.when(lower)
        def _():
            for a in range(2):
                for r in range(chunks):
                    sum_arrival(a, r, passed_from, core).wait_recv()
                    sum_copy(PASSED, a, r).start()

        for r in range(1, last):
            for a in range(2):
                pass_sum(a, r, upper)
            for a in range(2):
                read(a, r)
        for a in range(2):
            pass_sum(a, 0, upper)
        read(0, 0)
        pass_sum(0, last, upper)
        read(1, 0)
        pass_sum(1, last, upper)
        read(0, last)
        finish(0)
        read(1, last)
        finish(1)

    with scope("S_sends"):
        for kind in range(6):

            @pl.when(pass_out if kind == PASSED else exists[kind])
            def _(kind=kind):
                remote(green, green, sent.at[kind], raw_recv.at[0, 0], OWN).wait_send()

        for r in detours_raw:

            @pl.when(relayed(r))
            def _(r=r):
                raw_relay(r).wait_send()

        for r in detours_sum:

            @pl.when(relayed_sum(r))
            def _(r=r):
                for a in range(2):
                    sum_relay(a, r).wait_send()


def solution(mesh):
    energy_devices, atom_devices = mesh.shape["energy"], mesh.shape["atom"]

    def on_device(
        green_blocks, coupling, up_partner, down_partner, up_weight, down_weight, neighbours, strength
    ):
        orbitals = green_blocks.shape[-1]
        rows = orbitals // CHUNKS
        slots = neighbours.shape[1]
        clusters = neighbours.shape[0]

        def vmem(*shape, dtype=BF16):
            return pltpu.VMEM(shape, dtype)

        many = range(CHUNKS)
        scratch = (
            [vmem(8, 2, rows, orbitals) for _ in many]
            + [vmem(2, 2, 2, rows, orbitals) for _ in many]
            + [vmem(8, rows, orbitals) for _ in range(2 * CHUNKS)]
            + [vmem(2, 2, rows, orbitals) for _ in range(2 * CHUNKS)]
            + [vmem(2, rows, orbitals) for _ in range(2 * CHUNKS)]
            + [vmem(2, 2, rows, orbitals) for _ in many]
            + [vmem(2, 2, rows, orbitals) for _ in range(2)]
            + [vmem(2, rows, orbitals) for _ in range(4)]
            + [vmem(2, 2, rows, orbitals) for _ in range(2 * CHUNKS)]
            + [
                vmem(2, 2, 2, orbitals, orbitals),
                vmem(2, orbitals, orbitals),
                pltpu.SMEM((2,), jnp.int32),
                pltpu.SMEM((2,), jnp.int32),
                pltpu.SMEM((2,), F32),
                pltpu.SMEM((2,), F32),
                pltpu.SMEM((slots, clusters), jnp.int32),
                pltpu.SMEM((slots, clusters), F32),
                vmem(2, 2, rows, 2 * orbitals),
                vmem(2, 2, 2 * orbitals, 2 * orbitals),
                vmem(2, 2, orbitals, 2 * orbitals),
                vmem(2, 2, 2 * orbitals, 2 * orbitals),
                vmem(2, 2 * orbitals, 2 * orbitals),
                vmem(2, orbitals, 2 * orbitals, dtype=F32),
                pltpu.SemaphoreType.DMA((6,)),
                pltpu.SemaphoreType.DMA((4, CHUNKS)),
                pltpu.SemaphoreType.DMA((4, 2 * CHUNKS)),
                pltpu.SemaphoreType.DMA((6,)),
                pltpu.SemaphoreType.DMA((6,)),
                pltpu.SemaphoreType.DMA((8,)),
                pltpu.SemaphoreType.REGULAR,
            ]
        )
        return pl.pallas_call(
            functools.partial(kernel, energy_devices, atom_devices),
            out_shape=jax.ShapeDtypeStruct(green_blocks.shape, green_blocks.dtype),
            in_specs=[pl.BlockSpec(memory_space=pl.ANY)] * 8,
            out_specs=pl.BlockSpec(memory_space=pltpu.VMEM),
            scratch_shapes=scratch,
            compiler_params=pltpu.CompilerParams(
                collective_id=0, has_side_effects=True, vmem_limit_bytes=24 * 1024 * 1024
            ),
            name="update",
        )(
            *(
                pltpu.with_memory_space_constraint(array, pltpu.HBM)
                for array in (
                    green_blocks,
                    coupling,
                    up_partner,
                    down_partner,
                    up_weight,
                    down_weight,
                    neighbours.T,
                    strength.T,
                )
            )
        )

    in_specs = (
        P("energy", "atom", None, None, None),
        P("atom", None, None),
        P("energy"),
        P("energy"),
        P("energy"),
        P("energy"),
        P(),
        P(),
    )
    out_specs = P("energy", "atom", None, None, None)
    return jax.shard_map(
        on_device, mesh=mesh, in_specs=in_specs, out_specs=out_specs, check_vma=False
    )
```
